128 devices in a mesh: grp: 4 (over x), dev: 32 (over z, y, core).
Axes of the slice: x: 4, y: 4, z: 4, core: 2. Of those that a mesh axis runs over, the one named last changes fastest.
Arguments:
- memory: bfloat16 [262144, 512], P(('grp', 'dev')), may hold values from -6 to 6
- event_nodes: int32 [16384, 2], P(('grp', 'dev')), may hold values from 0 to 262143, as said below
- event_ticks: int32 [16384], P(('grp', 'dev')), may hold values from 0 to 99999
- neighbour_ids: int32 [16384, 20], P(('grp', 'dev')), may hold values from 0 to 262143, as said below
- neighbour_ticks: int32 [16384, 20], P(('grp', 'dev')), may hold values from 0 to 99999
- freq: float32 [128], replicated, may hold values from 1e-05 to 1
- phase: float32 [128], replicated, may hold values from -3.140625 to 3.140625
- w_msg1: bfloat16 [1152, 1024], replicated, may hold values from -0.1875 to 0.1875
- b_msg1: float32 [1024], replicated, may hold values from -3 to 3
- w_msg2: bfloat16 [1024, 512], replicated, may hold values from -0.1875 to 0.1875
- b_msg2: float32 [512], replicated, may hold values from -3 to 3
- w_query: bfloat16 [512, 512], replicated, may hold values from -1 to 1
- w_keyval: bfloat16 [640, 1024], replicated, may hold values from -1 to 1
- w_out: bfloat16 [512, 512], replicated, may hold values from -0.25 to 0.25
- gru_input: bfloat16 [512, 1536], replicated, may hold values from -0.25 to 0.25
- gru_hidden: bfloat16 [512, 1536], replicated, may hold values from -0.25 to 0.25
- gru_bias: float32 [2, 1536], replicated, may hold values from -3 to 3
Outputs:
- embedding: bfloat16 [16384, 512], P(('grp', 'dev'))
- new_memory: bfloat16 [262144, 512], P(('grp', 'dev'))
The draws below stay inside these ranges and needn't reach their ends.
Inputs may be any that keep to these rules, and one draw needn't show every extreme that they name: `event_nodes`: node n is held by device n // 2048 of the grp-major order; of the 256 ids of one device's events, at most 4 belong to any one owner device. `neighbour_ids`: of the 2560 neighbour ids of one device's events, at most 40 belong to any one owner device.
All inputs are finite; a program needn't handle non-finite values.
Results may differ from the reference program's by a relative error of at most 0.01.
Values may be sent and summed in bfloat16 or wider, within the bound.
No kernel may reach another device: no remote copies, remote signals or barrier semaphores. Data moves between devices by JAX's collectives and lax.ppermute only.
A program may use at most 128 MiB of HBM per device.

```python
import math
import jax
import jax.numpy as jnp
from jax import lax

D = 512
HID = 1024
TD = 128
K = 20
HDIM = 128
EV_DEV = 128
NODE_DEV = 2048
EVENTS = 16384
NODES = 262144
CAP_E = 4
CAP_N = 40
DEVICES = 128


def owned_ids(key, salt, columns, capacity, first_row, marked):
    total = DEVICES * capacity
    count = EV_DEV * columns
    id_key = jax.random.fold_in(key, salt)
    hottest = jax.random.randint(jax.random.fold_in(id_key, 7), (), 0, DEVICES)
    owners_pool = jnp.arange(total, dtype=jnp.int32) // capacity
    specials = jax.random.randint(jax.random.fold_in(key, 303), (DEVICES,), 0, EV_DEV)
    row_index = jnp.arange(EV_DEV, dtype=jnp.int32)[:, None]
    col_index = jnp.arange(columns, dtype=jnp.int32)[None, :]

    def one_device(dkey, special):
        ranking = jax.random.permutation(jax.random.fold_in(dkey, 1), total).astype(jnp.int32)
        flagged = jnp.where(owners_pool == hottest, 0, 1).astype(jnp.int32)
        order = jnp.argsort(flagged * total + ranking)
        chosen = owners_pool[order[:count]]
        chosen = chosen[jax.random.permutation(jax.random.fold_in(dkey, 2), count)].reshape(EV_DEV, columns)
        local_rows = jax.random.randint(jax.random.fold_in(dkey, 3), (EV_DEV, columns), 0, NODE_DEV)
        hit = jnp.logical_and(row_index == special, col_index < marked)
        local_rows = jnp.where(hit, first_row + col_index, local_rows)
        return (chosen * NODE_DEV + local_rows).astype(jnp.int32)
    dkeys = jax.random.split(jax.random.fold_in(id_key, 11), DEVICES)
    return jax.vmap(one_device)(dkeys, specials).reshape(EVENTS, columns)


def draw_event_nodes(key, part):
    return owned_ids(key, 101, 2, CAP_E, 0, 1)


def draw_neighbour_ids(key, part):
    return owned_ids(key, 202, K, CAP_N, 1, 2)


def draw_memory(key, part):
    values = jax.random.truncated_normal(jax.random.fold_in(key, 41), -6.0, 6.0, (NODES, D), jnp.float32)
    return values.astype(jnp.bfloat16)


def draw_w_query(key, part):
    values = jax.random.truncated_normal(jax.random.fold_in(key, 61), -6.0, 6.0, (D, D), jnp.float32) / jnp.sqrt(jnp.float32(D))
    return values.astype(jnp.bfloat16)


def draw_w_keyval(key, part):
    values = jax.random.truncated_normal(jax.random.fold_in(key, 62), -6.0, 6.0, (D + TD, 2 * D), jnp.float32) / jnp.sqrt(jnp.float32(D + TD))
    return values.astype(jnp.bfloat16)


def touch_ends(drawn, rng, low, top_value):
    longest = drawn.shape.index(max(drawn.shape))
    spots = []
    for shift in (0, 1):
        where = [jax.random.randint(jax.random.fold_in(rng, axis), (), 0, length) for axis, length in enumerate(drawn.shape)]
        where[longest] = (where[longest] + shift) % drawn.shape[longest]
        spots.append(tuple(where))
    return drawn.at[spots[0]].set(low).at[spots[1]].set(top_value)


def normal_values(key, shape, deviation, limit, kind=jnp.bfloat16):
    return jnp.clip(deviation * jax.random.normal(key, shape, jnp.float32), -limit, limit).astype(kind)


def setup_inputs(seed: int = 0) -> dict:
    key_list = jax.random.split(jax.random.key(seed), 18)
    memory = draw_memory(jax.random.fold_in(key_list[17], 71), 0)
    event_nodes = draw_event_nodes(jax.random.fold_in(key_list[17], 71), 0)
    event_ticks = touch_ends(jax.random.randint(key_list[2], (EVENTS,), 0, 100000), jax.random.fold_in(key_list[2], 1), 0, 99999).astype(jnp.int32)
    neighbour_ids = draw_neighbour_ids(jax.random.fold_in(key_list[17], 71), 0)
    neighbour_ticks = touch_ends(jax.random.randint(key_list[4], (EVENTS, K), 0, 100000), jax.random.fold_in(key_list[4], 1), 0, 99999).astype(jnp.int32)
    freq = jnp.clip(jnp.exp(jax.random.uniform(key_list[5], (TD,), jnp.float32, math.log(9.999999747378752e-06), math.log(1.0))), 9.999999747378752e-06, 1.0)
    phase = jnp.clip(jax.random.uniform(key_list[6], (TD,), jnp.float32, -3.140625, 3.140625), -3.140625, 3.140625)
    w_msg1 = normal_values(key_list[7], (2 * D + TD, HID), (2 * D + TD) ** -0.5, 0.1875)
    b_msg1 = normal_values(key_list[8], (HID,), 0.5, 3.0, jnp.float32)
    w_msg2 = normal_values(key_list[9], (HID, D), HID ** -0.5, 0.1875)
    b_msg2 = normal_values(key_list[10], (D,), 0.5, 3.0, jnp.float32)
    w_query = draw_w_query(jax.random.fold_in(key_list[17], 71), 0)
    w_keyval = draw_w_keyval(jax.random.fold_in(key_list[17], 71), 0)
    w_out = normal_values(key_list[13], (D, D), D ** -0.5, 0.25)
    gru_input = normal_values(key_list[14], (D, 3 * D), D ** -0.5, 0.25)
    gru_hidden = normal_values(key_list[15], (D, 3 * D), D ** -0.5, 0.25)
    gru_bias = normal_values(key_list[16], (2, 3 * D), 0.5, 3.0, jnp.float32)
    return {"memory": memory, "event_nodes": event_nodes, "event_ticks": event_ticks, "neighbour_ids": neighbour_ids, "neighbour_ticks": neighbour_ticks, "freq": freq, "phase": phase, "w_msg1": w_msg1, "b_msg1": b_msg1, "w_msg2": w_msg2, "b_msg2": b_msg2, "w_query": w_query, "w_keyval": w_keyval, "w_out": w_out, "gru_input": gru_input, "gru_hidden": gru_hidden, "gru_bias": gru_bias}


def encode(ticks, freq, phase):
    return jnp.cos(ticks.astype(jnp.float32)[..., None] * freq + phase).astype(jnp.bfloat16)

def message_net(inputs, w_msg1, b_msg1, w_msg2, b_msg2):
    hidden = jnp.maximum(jnp.dot(inputs, w_msg1, preferred_element_type=jnp.float32) + b_msg1, 0.0).astype(jnp.bfloat16)
    return (jnp.dot(hidden, w_msg2, preferred_element_type=jnp.float32) + b_msg2).astype(jnp.bfloat16)

def gru_cell(mean, state, gru_input, gru_hidden, gru_bias):
    width = state.shape[1]
    gate_in = jnp.dot(mean, gru_input, preferred_element_type=jnp.float32) + gru_bias[0]
    gate_hid = jnp.dot(state, gru_hidden, preferred_element_type=jnp.float32) + gru_bias[1]
    reset = jax.nn.sigmoid(gate_in[:, :width] + gate_hid[:, :width])
    update = jax.nn.sigmoid(gate_in[:, width:2 * width] + gate_hid[:, width:2 * width])
    candidate = jnp.tanh(gate_in[:, 2 * width:] + reset * gate_hid[:, 2 * width:])
    return (1.0 - update) * candidate + update * state.astype(jnp.float32)

def attend(m_self, m_near, dt_enc, w_query, w_keyval, w_out):
    count, fanout, width = m_near.shape
    heads = width // HDIM
    query = jnp.dot(m_self, w_query, preferred_element_type=jnp.float32).astype(jnp.bfloat16).reshape(count, heads, HDIM)
    feats = jnp.concatenate([m_near, dt_enc], axis=-1).reshape(count * fanout, -1)
    keyval = jnp.dot(feats, w_keyval, preferred_element_type=jnp.float32).astype(jnp.bfloat16).reshape(count, fanout, 2, heads, HDIM)
    scores = jnp.einsum('ehc,ekhc->ehk', query.astype(jnp.float32), keyval[:, :, 0].astype(jnp.float32)) / jnp.sqrt(jnp.float32(HDIM))
    scores = scores - lax.optimization_barrier(jnp.max(scores, axis=-1, keepdims=True))
    expo = jnp.exp(scores)
    weights = (expo / lax.optimization_barrier(jnp.sum(expo, axis=-1, keepdims=True))).astype(jnp.bfloat16)
    attn = jnp.einsum('ehk,ekhc->ehc', weights.astype(jnp.float32), keyval[:, :, 1].astype(jnp.float32)).astype(jnp.bfloat16).reshape(count, width)
    return jnp.dot(attn, w_out, preferred_element_type=jnp.float32).astype(jnp.bfloat16)

def reference(memory, event_nodes, event_ticks, neighbour_ids, neighbour_ticks, freq, phase, w_msg1, b_msg1, w_msg2, b_msg2, w_query, w_keyval, w_out, gru_input, gru_hidden, gru_bias):
    nodes, width = memory.shape
    src = event_nodes[:, 0]
    dst = event_nodes[:, 1]
    m_src = memory[src]
    m_dst = memory[dst]
    enc = encode(event_ticks, freq, phase)
    msg_src = message_net(jnp.concatenate([m_src, m_dst, enc], axis=1), w_msg1, b_msg1, w_msg2, b_msg2)
    msg_dst = message_net(jnp.concatenate([m_dst, m_src, enc], axis=1), w_msg1, b_msg1, w_msg2, b_msg2)
    sums = jnp.zeros((nodes, width), jnp.float32).at[src].add(msg_src.astype(jnp.float32)).at[dst].add(msg_dst.astype(jnp.float32))
    counts = jnp.zeros((nodes,), jnp.float32).at[src].add(1.0).at[dst].add(1.0)
    mean = (sums / jnp.maximum(counts, 1.0)[:, None]).astype(jnp.bfloat16)
    blocks = nodes // NODE_DEV

    def update_block(args):
        mean_block, state_block, count_block = args
        fresh = gru_cell(mean_block, state_block, gru_input, gru_hidden, gru_bias)
        return jnp.where(count_block[:, None] > 0.0, fresh, state_block.astype(jnp.float32)).astype(jnp.bfloat16)
    new_memory = lax.map(update_block, (mean.reshape(blocks, NODE_DEV, width), memory.reshape(blocks, NODE_DEV, width), counts.reshape(blocks, NODE_DEV))).reshape(nodes, width)
    events = event_nodes.shape[0]
    eblocks = events // EV_DEV

    def embed_block(args):
        self_block, near_ids, ticks_block, near_ticks = args
        m_near = memory[near_ids]
        dt_enc = encode(ticks_block[:, None] - near_ticks, freq, phase)
        return attend(self_block, m_near, dt_enc, w_query, w_keyval, w_out)
    embedding = lax.map(embed_block, (m_src.reshape(eblocks, EV_DEV, width), neighbour_ids.reshape(eblocks, EV_DEV, -1), event_ticks.reshape(eblocks, EV_DEV), neighbour_ticks.reshape(eblocks, EV_DEV, -1))).reshape(events, width)
    return (embedding, new_memory)
```

```python
import functools

import jax
import jax.numpy as jnp
from jax import lax
from jax.experimental import pallas as pl
from jax.experimental.pallas import tpu as pltpu
from jax.sharding import PartitionSpec as P

HDIM = 128
LANES = 128
AXES = ("grp", "dev")
F32 = jnp.float32
BF16 = jnp.bfloat16
NEG = -1e30
NT = (((1,), (1,)), ((), ()))


def dotf(a, b):
    return jnp.dot(a, b, preferred_element_type=F32)


def exchange(x):
    return lax.all_to_all(x, AXES, split_axis=0, concat_axis=0, tiled=True)


def call(kernel, out_shape, *args, scalars=0, scratch=(), mib=16):
    return pl.pallas_call(
        kernel,
        out_shape=out_shape,
        grid_spec=pltpu.PrefetchScalarGridSpec(
            num_scalar_prefetch=scalars,
            grid=(),
            in_specs=[pl.BlockSpec(memory_space=pltpu.VMEM)] * (len(args) - scalars),
            out_specs=jax.tree.map(lambda _: pl.BlockSpec(memory_space=pltpu.VMEM), out_shape),
            scratch_shapes=scratch,
        ),
        compiler_params=pltpu.CompilerParams(vmem_limit_bytes=mib << 20),
    )(*args)


def hbm(x):
    return pltpu.with_memory_space_constraint(x, pltpu.HBM)


def vmem(x):
    return pltpu.with_memory_space_constraint(x, pltpu.VMEM)


def whole(x):
    zeros = (0,) * x.ndim
    return pl.BlockSpec(x.shape, lambda *_: zeros)


def sds(shape, dtype):
    return jax.ShapeDtypeStruct(shape, dtype)


def place_kernel(shift, cap_n, cap_e, rows, nid_ref, nt_ref, en_ref, tick_ref, req_ref, map_ref, dt_ref):
    fanout, events = nid_ref.shape
    owners = req_ref.shape[0]
    i0 = lax.broadcasted_iota(jnp.int32, (owners, events), 0)
    e0 = lax.broadcasted_iota(jnp.int32, (events, events), 0)
    e1 = lax.broadcasted_iota(jnp.int32, (events, events), 1)
    tri = jnp.where(e0 <= e1, 1.0, 0.0)
    both = jnp.concatenate([tri, jnp.ones((events, events), F32)], axis=1).astype(BF16)
    srow = lax.broadcasted_iota(jnp.int32, (rows, events), 0)
    lane = lax.broadcasted_iota(jnp.int32, (1, events), 1)
    tick = tick_ref[...]
    mask = (1 << shift) - 1
    acc = jnp.zeros((6 * rows, owners), F32)
    base = jnp.zeros((owners, events), F32)
    zero = jnp.zeros((1, events), jnp.int32)
    for k in range(fanout + 2):
        near = k < fanout
        if k == fanout:
            base = jnp.zeros((owners, events), F32)
        ids = nid_ref[k : k + 1, :] if near else en_ref[k - fanout : k - fanout + 1, :]
        local = jnp.bitwise_and(ids, mask)
        hit = i0 == jnp.right_shift(ids, shift)
        onehot = jnp.where(hit, 1.0, 0.0)
        ohb = onehot.astype(BF16)
        ranks = dotf(ohb, both)
        cum = ranks[:, :events] + base
        base = base + ranks[:, events:]
        slot = jnp.sum(onehot * cum, axis=0, keepdims=True).astype(jnp.int32) - 1
        if near:
            d = tick - nt_ref[k : k + 1, :] + 131072
            code = lane + 1
            parts = (d & 255, jnp.right_shift(d, 8) & 255, jnp.right_shift(d, 16))
            value = local
        else:
            slot = slot + cap_n
            code = lane + (1 + events * (k - fanout))
            parts = (zero, zero, zero)
            value = local + 1
        vals = (value & 255, jnp.right_shift(value, 8), code) + parts
        so = srow == slot
        table = jnp.concatenate([jnp.where(so, v.astype(F32), 0.0) for v in vals], axis=0)
        acc = acc + lax.dot_general(table.astype(BF16), ohb, NT, preferred_element_type=F32)
    a = [acc[i * rows : (i + 1) * rows] for i in range(6)]
    pad = jnp.zeros((LANES - rows, owners), F32)

    def turned(x):
        return jnp.concatenate([x, pad], axis=0).T

    req_ref[...] = turned(a[0] + 256.0 * a[1]).astype(jnp.int32)
    map_ref[...] = turned(a[2]).astype(jnp.int32)
    dt = a[3] + 256.0 * a[4] + 65536.0 * a[5] - 131072.0
    dt_ref[...] = turned(jnp.where(a[2] > 0.0, dt, 0.0))


def spread_kernel(mem_ref, out_ref):
    nodes, width = mem_ref.shape
    parts = width // LANES
    block = 128

    def step(i, carry):
        r = pl.multiple_of(i * block, block)
        for c in range(parts):
            part = mem_ref[pl.ds(r, block), c * LANES : (c + 1) * LANES].astype(F32)
            out_ref[pl.ds(r * parts + c, block, stride=parts), :] = part
        return carry

    lax.fori_loop(0, nodes // block, step, 0)


def pick_kernel(cols, shifted, req_ref, mem_ref, out_ref, stage_ref):
    n = len(cols)
    parts = stage_ref.shape[0] // 32
    group = 16 // n if n < 16 else 1
    total = n * group
    steps = out_ref.shape[0] // total
    start = pl.program_id(0) * (out_ref.shape[0] // n)

    def step(i, carry):
        for g in range(group):
            o = start + i * group + g
            for j, col in enumerate(cols):
                row = req_ref[o, col]
                if shifted[j]:
                    row = jnp.maximum(row - 1, 0)
                at = pl.multiple_of(row * parts, parts)
                s = (g * n + j) * parts
                stage_ref[s : s + parts, :] = mem_ref[pl.ds(at, parts), :]
        r = pl.multiple_of(i * total, total)
        for c in range(parts):
            part = stage_ref[pl.ds(c, total, stride=parts), :]
            out_ref[pl.ds(r, total), c * LANES : (c + 1) * LANES] = part.astype(BF16)
        return carry

    lax.fori_loop(0, steps, step, 0)


def pick(req, mem32, width, cols, shifted):
    peers = req.shape[0]
    parts = width // LANES
    rows = peers * len(cols)
    blocks = 4
    return pl.pallas_call(
        functools.partial(pick_kernel, cols, shifted),
        out_shape=pltpu.HBM((rows, width), BF16),
        grid_spec=pltpu.PrefetchScalarGridSpec(
            num_scalar_prefetch=1,
            grid=(blocks,),
            in_specs=[pl.BlockSpec(memory_space=pltpu.VMEM)],
            out_specs=pl.BlockSpec((rows // blocks, width), lambda i, _: (i, 0)),
            scratch_shapes=[pltpu.VMEM((32 * parts, LANES), F32)],
        ),
        compiler_params=pltpu.CompilerParams(vmem_limit_bytes=8 << 20),
    )(hbm(req), vmem(mem32))


def message_kernel(cap_e, rows_ref, base_ref, code_ref, enc_ref, w1_ref, b1_ref, w2_ref, b2_ref, wq_ref, out_ref, q_ref):
    peers, per, width = rows_ref.shape
    slots = peers * per
    events = enc_ref.shape[0]
    code = code_ref[...]
    target = lax.broadcasted_iota(jnp.int32, (2 * events, slots), 0) + 1
    sel = jnp.where(target == code, 1.0, 0.0)
    rows = rows_ref[...].reshape(slots, width)
    pair = dotf(sel.astype(BF16), rows).astype(BF16)
    q_ref[...] = dotf(pair[:events], wq_ref[...]).astype(BF16)
    first = dotf(pair, w1_ref[:width, :])
    second = dotf(pair, w1_ref[width : 2 * width, :])
    third = dotf(enc_ref[...], w1_ref[2 * width :, :])
    both = jnp.concatenate([second[events:] + third, second[:events] + third], axis=0)
    hidden = jnp.maximum(first + both + b1_ref[...], 0.0).astype(BF16)
    msg = (dotf(hidden, w2_ref[...]) + b2_ref[...]).astype(BF16)
    placed = dotf(sel.T.astype(BF16), msg)
    j = lax.broadcasted_iota(jnp.int32, (slots, width), 0) & (per - 1)
    base = base_ref[...].reshape(slots, width).astype(F32)
    out = jnp.where(j < cap_e, placed, base).astype(BF16)
    out_ref[...] = out.reshape(peers, per, width)


def messages(cap_e, got, base, code, enc, *weights):
    peers, _, width = got.shape
    tile = pl.BlockSpec((peers, 8, width), lambda i: (0, 0, 0))
    args = (hbm(got), hbm(base), code, enc, *weights)
    q_shape = sds((enc.shape[0], width), BF16)
    return pl.pallas_call(
        functools.partial(message_kernel, cap_e),
        out_shape=(pltpu.HBM(base.shape, BF16), q_shape),
        grid=(1,),
        in_specs=[tile, tile] + [whole(x) for x in args[2:]],
        out_specs=(tile, whole(q_shape)),
        input_output_aliases={1: 0},
        compiler_params=pltpu.CompilerParams(vmem_limit_bytes=24 << 20),
    )(*args)


def gru_kernel(msgs_ref, old_ref, gh_ref, to_c_ref, to_t_ref, mem_ref, wi_ref, bias_ref, out_ref, fresh_ref, lead_ref):
    peers, per, width = msgs_ref.shape
    slots = old_ref.shape[0]
    block = mem_ref.shape[0]
    step = pl.program_id(0)

    @pl.when(step == 0)
    def _():
        row = to_c_ref[...].astype(F32)
        col = jnp.broadcast_to(row, (8, slots)).T[:, 0:1]
        tiles = to_t_ref[...].astype(F32)
        hits = jnp.where(jnp.logical_and(col == tiles, tiles > 0.0), 1.0, 0.0)
        counts = jnp.sum(hits, axis=1, keepdims=True)
        sums = dotf(hits.astype(BF16), msgs_ref[...].reshape(peers * per, width))
        mean = (sums / jnp.maximum(counts, 1.0)).astype(BF16)
        s0 = lax.broadcasted_iota(jnp.int32, (slots, slots), 0)
        s1 = lax.broadcasted_iota(jnp.int32, (slots, slots), 1)
        same = jnp.logical_and(col == row, s0 < s1)
        earlier = jnp.max(jnp.where(same, 1.0, 0.0), axis=0, keepdims=True)
        lead_ref[...] = jnp.where(earlier > 0.0, 0.0, row)
        old = old_ref[...].astype(F32)
        gi = dotf(mean, wi_ref[...]) + bias_ref[0:1, :]
        gh = gh_ref[...]
        r = jax.nn.sigmoid(gi[:, :width] + gh[:, :width])
        z = jax.nn.sigmoid(gi[:, width : 2 * width] + gh[:, width : 2 * width])
        c = jnp.tanh(gi[:, 2 * width :] + r * gh[:, 2 * width :])
        fresh_ref[...] = ((1.0 - z) * c + z * old).astype(BF16)

    node = lax.broadcasted_iota(jnp.int32, (block, slots), 0) + (step * block + 1)
    hit = jnp.where(node.astype(F32) == lead_ref[...], 1.0, 0.0)
    reached = jnp.max(hit, axis=1, keepdims=True)
    new = dotf(hit.astype(BF16), fresh_ref[...])
    out_ref[...] = jnp.where(reached > 0.0, new, mem_ref[...].astype(F32)).astype(BF16)


def update(got, old, gh, to_c, to_t, memory, wi, bias):
    peers, _, width = got.shape
    nodes = memory.shape[0]
    slots = old.shape[0]
    block = 512
    tile = pl.BlockSpec((peers, 8, width), lambda i: (0, 0, 0))
    part = pl.BlockSpec((block, width), lambda i: (i, 0))
    return pl.pallas_call(
        gru_kernel,
        out_shape=sds(memory.shape, BF16),
        grid=(nodes // block,),
        in_specs=[tile] + [whole(x) for x in (old, gh, to_c, to_t)] + [part, whole(wi), whole(bias)],
        out_specs=part,
        scratch_shapes=[pltpu.VMEM((slots, width), BF16), pltpu.VMEM((1, slots), F32)],
        compiler_params=pltpu.CompilerParams(vmem_limit_bytes=28 << 20),
    )(hbm(got), hbm(old), hbm(gh), to_c, to_t, hbm(memory), wi, bias)


def attend_kernel(first, last, *refs):
    rows_ref, enc_ref, map_ref, q_ref, w_ref = refs[:5]
    at = 5
    if not first:
        start = refs[at : at + 3]
        at += 3
    if last:
        wo_ref, out_ref, m_ref, l_ref, a_ref = refs[at:]
    else:
        m_ref, l_ref, a_ref = refs[at:]
    step = pl.program_id(0)
    slots, width = rows_ref.shape
    events = q_ref.shape[0]
    heads = width // HDIM

    @pl.when(step == 0)
    def _():
        if first:
            m_ref[...] = jnp.full((events, width), NEG, F32)
            l_ref[...] = jnp.zeros((events, width), F32)
            a_ref[...] = jnp.zeros((events, width), F32)
        else:
            for dst, src in zip((m_ref, l_ref, a_ref), start):
                dst[...] = src[...]

    kv = dotf(rows_ref[...], w_ref[:width, :]) + dotf(enc_ref[...], w_ref[width:, :])
    kv = kv.astype(BF16)
    event = lax.broadcasted_iota(jnp.int32, (events, slots), 0) + 1
    mine = event == map_ref[...]
    for h in range(heads):
        cut = slice(h * HDIM, (h + 1) * HDIM)
        s = lax.dot_general(q_ref[:, cut], kv[:, cut], NT, preferred_element_type=F32)
        s = jnp.where(mine, s * (1.0 / HDIM**0.5), NEG)
        m_old = m_ref[:, cut]
        m = jnp.maximum(m_old, jnp.max(s, axis=1, keepdims=True))
        p = jnp.where(mine, jnp.exp(s - m[:, 0:1]), 0.0)
        scale = jnp.exp(m_old - m)
        m_ref[:, cut] = m
        l_ref[:, cut] = scale * l_ref[:, cut] + jnp.sum(p, axis=1, keepdims=True)
        add = dotf(p.astype(BF16), kv[:, width + h * HDIM : width + (h + 1) * HDIM])
        a_ref[:, cut] = scale * a_ref[:, cut] + add

    if last:

        @pl.when(step == pl.num_programs(0) - 1)
        def _():
            attn = (a_ref[...] / l_ref[...]).astype(BF16)
            out_ref[...] = dotf(attn, wo_ref[...]).astype(BF16)


def attend(rows, enc, slot_map, query, w, state=None, w_out=None):
    first, last = state is None, w_out is not None
    total, width = rows.shape
    events = query.shape[0]
    block = 1024
    shapes = tuple(pltpu.VMEM((events, width), F32) for _ in range(3))
    kept = tuple(vmem(x) for x in state) if state else ()
    args = (hbm(rows), hbm(enc), slot_map, query, w) + kept + ((w_out,) if last else ())
    in_specs = [
        pl.BlockSpec((block, width), lambda i: (i, 0)),
        pl.BlockSpec((block, LANES), lambda i: (i, 0)),
        pl.BlockSpec((1, block), lambda i: (0, i)),
    ] + [whole(x) for x in args[3:]]
    final = sds((events, width), BF16)
    return pl.pallas_call(
        functools.partial(attend_kernel, first, last),
        out_shape=final if last else shapes,
        grid=(total // block,),
        in_specs=in_specs,
        out_specs=whole(final) if last else tuple(whole(final) for _ in shapes),
        scratch_shapes=[pltpu.VMEM((events, width), F32)] * 3 if last else [],
        compiler_params=pltpu.CompilerParams(vmem_limit_bytes=24 << 20),
    )(*args)


def encode(dt, freq, phase):
    return jnp.cos(dt[..., None] * freq + phase).astype(BF16)


def on_device(
    memory,
    event_nodes,
    event_ticks,
    neighbour_ids,
    neighbour_ticks,
    freq,
    phase,
    w_msg1,
    b_msg1,
    w_msg2,
    b_msg2,
    w_query,
    w_keyval,
    w_out,
    gru_input,
    gru_hidden,
    gru_bias,
):
    owners = lax.axis_size(AXES)
    nodes, width = memory.shape
    events, fanout = neighbour_ids.shape
    cap_e = 4 * events // owners
    cap_n = 2 * fanout * events // owners
    rows = cap_n + 8
    shift = nodes.bit_length() - 1
    assert nodes == 1 << shift and cap_e == 4 and cap_n == 40
    table = (owners, LANES)
    req, owner_map, dt = call(
        functools.partial(place_kernel, shift, cap_n, cap_e, rows),
        (sds(table, jnp.int32), sds(table, jnp.int32), sds(table, F32)),
        hbm(neighbour_ids.T),
        hbm(neighbour_ticks.T),
        hbm(event_nodes.T),
        hbm(event_ticks.reshape(1, events)),
        mib=8,
    )
    mem32 = call(spread_kernel, pltpu.VMEM((nodes * width // LANES, LANES), F32), hbm(memory), mib=8)
    asked = exchange(req)

    half = 8 - cap_e
    near = 28
    ev = tuple(range(cap_n, cap_n + cap_e))
    cols_a = ev + tuple(range(near))
    cols_c = tuple(range(near, near + cap_e)) + tuple(range(near, cap_n))
    take = functools.partial(pick, asked, mem32, width)
    sent_a = take(cols_a, (True,) * cap_e + (False,) * near)
    got_a = exchange(sent_a)
    base_c = take(cols_c, (False,) * len(cols_c)).reshape(owners, -1, width)
    old = take(ev, (True,) * cap_e)

    def spaced(x, width):
        return jnp.concatenate([jnp.zeros((owners, width), x.dtype), x], axis=1)

    def tiled(x):
        return jnp.concatenate([x, jnp.zeros((owners, half), x.dtype)], axis=1).reshape(1, -1)

    code = tiled(owner_map[:, cap_n : cap_n + cap_e])
    map_a = spaced(owner_map[:, :near], cap_e).reshape(1, -1)
    map_c = spaced(owner_map[:, near:cap_n], cap_e).reshape(1, -1)
    to = asked[:, cap_n : cap_n + cap_e]
    to_t = tiled(to)
    to_c = to.reshape(1, -1)
    gh = jnp.dot(old, gru_hidden, preferred_element_type=F32) + gru_bias[1]
    enc_a = encode(spaced(dt[:, :near], cap_e), freq, phase).reshape(-1, LANES)
    enc_c = encode(spaced(dt[:, near:cap_n], cap_e), freq, phase).reshape(-1, LANES)
    enc = encode(event_ticks.astype(F32), freq, phase)
    got_a, enc_a, enc_c, map_a, map_c, gh, old, to_c, to_t = lax.optimization_barrier(
        (got_a, enc_a, enc_c, map_a, map_c, gh, old, to_c, to_t)
    )
    sent_c, query = messages(
        cap_e,
        got_a.reshape(owners, -1, width),
        base_c,
        code,
        enc,
        w_msg1,
        b_msg1.reshape(1, -1),
        w_msg2,
        b_msg2.reshape(1, -1),
        w_query,
    )
    got_c = exchange(sent_c)
    state = attend(got_a, enc_a, map_a, query, w_keyval)
    new_memory = update(got_c, old, gh, to_c, to_t, memory, gru_input, gru_bias)
    embedding = attend(got_c.reshape(-1, width), enc_c, map_c, query, w_keyval, state, w_out)
    return (embedding, new_memory)


def solution(mesh):
    split = P(AXES, None)
    in_specs = (split, split, P(AXES), split, split) + (P(),) * 12
    return jax.shard_map(
        on_device, mesh=mesh, in_specs=in_specs, out_specs=(split, split), check_vma=False
    )
```

```python
import functools

import jax
import jax.numpy as jnp
from jax import lax
from jax.experimental import pallas as pl
from jax.experimental.pallas import tpu as pltpu
from jax.sharding import PartitionSpec as P

HDIM = 128
LANES = 128
AXES = ("grp", "dev")
F32 = jnp.float32
BF16 = jnp.bfloat16
NEG = -1e30
NT = (((1,), (1,)), ((), ()))


def dotf(a, b):
    return jnp.dot(a, b, preferred_element_type=F32)


def exchange(x):
    return lax.all_to_all(x, AXES, split_axis=0, concat_axis=0, tiled=True)


def call(kernel, out_shape, *args, scalars=0, scratch=(), mib=16):
    return pl.pallas_call(
        kernel,
        out_shape=out_shape,
        grid_spec=pltpu.PrefetchScalarGridSpec(
            num_scalar_prefetch=scalars,
            grid=(),
            in_specs=[pl.BlockSpec(memory_space=pltpu.VMEM)] * (len(args) - scalars),
            out_specs=jax.tree.map(lambda _: pl.BlockSpec(memory_space=pltpu.VMEM), out_shape),
            scratch_shapes=scratch,
        ),
        compiler_params=pltpu.CompilerParams(vmem_limit_bytes=mib << 20),
    )(*args)


def hbm(x):
    return pltpu.with_memory_space_constraint(x, pltpu.HBM)


def vmem(x):
    return pltpu.with_memory_space_constraint(x, pltpu.VMEM)


def whole(x):
    zeros = (0,) * x.ndim
    return pl.BlockSpec(x.shape, lambda *_: zeros)


def sds(shape, dtype):
    return jax.ShapeDtypeStruct(shape, dtype)


def place_kernel(shift, parts, cap_n, rows, nid_ref, nt_ref, en_ref, tick_ref, req_ref, map_ref, dt_ref):
    fanout, events = nid_ref.shape
    owners = req_ref.shape[0]
    i0 = lax.broadcasted_iota(jnp.int32, (owners, events), 0)
    e0 = lax.broadcasted_iota(jnp.int32, (events, events), 0)
    e1 = lax.broadcasted_iota(jnp.int32, (events, events), 1)
    tri = jnp.where(e0 <= e1, 1.0, 0.0)
    both = jnp.concatenate([tri, jnp.ones((events, events), F32)], axis=1).astype(BF16)
    srow = lax.broadcasted_iota(jnp.int32, (rows, events), 0)
    lane = lax.broadcasted_iota(jnp.int32, (1, events), 1)
    tick = tick_ref[...]
    mask = (1 << shift) - 1
    acc = jnp.zeros((6 * rows, owners), F32)
    base = jnp.zeros((owners, events), F32)
    zero = jnp.zeros((1, events), jnp.int32)
    for k in range(fanout + 2):
        near = k < fanout
        if k == fanout:
            base = jnp.zeros((owners, events), F32)
        ids = nid_ref[k : k + 1, :] if near else en_ref[k - fanout : k - fanout + 1, :]
        local = jnp.bitwise_and(ids, mask)
        hit = i0 == jnp.right_shift(ids, shift)
        onehot = jnp.where(hit, 1.0, 0.0)
        ohb = onehot.astype(BF16)
        ranks = dotf(ohb, both)
        cum = ranks[:, :events] + base
        base = base + ranks[:, events:]
        slot = jnp.sum(onehot * cum, axis=0, keepdims=True).astype(jnp.int32) - 1
        if near:
            d = tick - nt_ref[k : k + 1, :] + 131072
            code = lane + 1
            digits = (d & 255, jnp.right_shift(d, 8) & 255, jnp.right_shift(d, 16))
            value = local * parts
        else:
            slot = slot + cap_n
            code = lane + (1 + events * (k - fanout))
            digits = (zero, zero, zero)
            value = (local + 1) * parts
        vals = (value & 255, jnp.right_shift(value, 8), code) + digits
        so = srow == slot
        table = jnp.concatenate([jnp.where(so, v.astype(F32), 0.0) for v in vals], axis=0)
        acc = acc + lax.dot_general(table.astype(BF16), ohb, NT, preferred_element_type=F32)
    a = [acc[i * rows : (i + 1) * rows] for i in range(6)]
    pad = jnp.zeros((LANES - rows, owners), F32)

    def turned(x):
        return jnp.concatenate([x, pad], axis=0).T

    req_ref[...] = turned(a[0] + 256.0 * a[1]).astype(jnp.int32)
    map_ref[...] = turned(a[2]).astype(jnp.int32)
    dt = a[3] + 256.0 * a[4] + 65536.0 * a[5] - 131072.0
    dt_ref[...] = turned(jnp.where(a[2] > 0.0, dt, 0.0))


def spread(src_ref, dst_ref, base=0):
    rows, width = src_ref.shape
    parts = width // LANES
    block = 128

    def step(i, carry):
        r = pl.multiple_of(i * block, block)
        for c in range(parts):
            part = src_ref[pl.ds(r, block), c * LANES : (c + 1) * LANES].astype(F32)
            dst_ref[pl.ds(base + r * parts + c, block, stride=parts), :] = part
        return carry

    lax.fori_loop(0, rows // block, step, 0)


def gather_back(src_ref, base, dst_ref, row, rows):
    parts = dst_ref.shape[1] // LANES
    for c in range(parts):
        part = src_ref[pl.ds(base + c, rows, stride=parts), :]
        dst_ref[pl.ds(row, rows), c * LANES : (c + 1) * LANES] = part.astype(dst_ref.dtype)


def pick_group(n):
    return 16 // n if n < 16 else 2


def pick_kernel(cols, shifted, req_ref, mem_ref, out_ref, req_s, mem_v, mem32, stage, out_v, sems):
    peers = req_ref.shape[0]
    width = mem_ref.shape[1]
    parts = width // LANES
    n = len(cols)
    blocks = out_v.shape[0]
    group = pick_group(n)
    total = n * group
    steps = peers // group // blocks
    load_mem = pltpu.make_async_copy(mem_ref, mem_v, sems.at[0])
    load_req = pltpu.make_async_copy(req_ref, req_s, sems.at[1])
    load_mem.start()
    load_req.start()
    load_mem.wait()
    spread(mem_v, mem32)
    load_req.wait()
    copies = []
    for b in range(blocks):

        def step(i, carry):
            for g in range(group):
                o = (b * steps + i) * group + g
                for j, col in enumerate(cols):
                    at = req_s[o, col]
                    if shifted[j]:
                        at = jnp.maximum(at - parts, 0)
                    at = pl.multiple_of(at, parts)
                    s = (g * n + j) * parts
                    stage[s : s + parts, :] = mem32[pl.ds(at, parts), :]
            r = pl.multiple_of(i * total, total)
            gather_back(stage, 0, out_v.at[b], r, total)
            return carry

        lax.fori_loop(0, steps, step, 0)
        size = steps * total
        copy = pltpu.make_async_copy(out_v.at[b], out_ref.at[pl.ds(b * size, size)], sems.at[2 + b])
        copy.start()
        copies.append(copy)
    for copy in copies:
        copy.wait()


def pick(req, memory, cols, shifted, blocks=4):
    peers = req.shape[0]
    nodes, width = memory.shape
    parts = width // LANES
    rows = peers * len(cols)
    anywhere = pl.BlockSpec(memory_space=pl.ANY)
    return pl.pallas_call(
        functools.partial(pick_kernel, cols, shifted),
        out_shape=pltpu.HBM((rows, width), BF16),
        in_specs=[anywhere, anywhere],
        out_specs=anywhere,
        scratch_shapes=[
            pltpu.SMEM(req.shape, jnp.int32),
            pltpu.VMEM((nodes, width), BF16),
            pltpu.VMEM((nodes * parts, LANES), F32),
            pltpu.VMEM((len(cols) * pick_group(len(cols)) * parts, LANES), F32),
            pltpu.VMEM((blocks, rows // blocks, width), BF16),
            pltpu.SemaphoreType.DMA((2 + blocks,)),
        ],
        compiler_params=pltpu.CompilerParams(vmem_limit_bytes=16 << 20),
    )(hbm(req), hbm(memory))


def starts(pairs, sems):
    copies = [pltpu.make_async_copy(src, dst, sems.at[i]) for i, (src, dst) in enumerate(pairs)]
    for copy in copies:
        copy.start()
    return copies


def message_kernel(cap_e, *refs):
    ins = refs[:9]
    out_ref, q_ref = refs[9:11]
    rows, code, w1, enc, b1, w2, b2, base, wq, out_v, q_v, sems = refs[11:]
    peers, per, width = rows.shape
    slots = peers * per
    events = enc.shape[0]
    sources = (ins[0].at[:, 0:per, :],) + tuple(ins[1:])
    loads = starts(list(zip(sources, (rows, code, w1, enc, b1, w2, b2, base, wq))), sems)
    loads[1].wait()
    target = lax.broadcasted_iota(jnp.int32, (2 * events, slots), 0) + 1
    sel = jnp.where(target == code[...], 1.0, 0.0)
    loads[0].wait()
    pair = dotf(sel.astype(BF16), rows[...].reshape(slots, width)).astype(BF16)
    for i in (2, 3, 4):
        loads[i].wait()
    first = dotf(pair, w1[:width, :])
    second = dotf(pair, w1[width : 2 * width, :])
    third = dotf(enc[...], w1[2 * width :, :]) + b1[...]
    both = jnp.concatenate([second[events:] + third, second[:events] + third], axis=0)
    hidden = jnp.maximum(first + both, 0.0).astype(BF16)
    for i in (5, 6):
        loads[i].wait()
    msg = (dotf(hidden, w2[...]) + b2[...]).astype(BF16)
    placed = dotf(sel.T.astype(BF16), msg)
    j = lax.broadcasted_iota(jnp.int32, (slots, width), 0) & (per - 1)
    loads[7].wait()
    kept = base[...].reshape(slots, width).astype(F32)
    out_v[...] = jnp.where(j < cap_e, placed, kept).astype(BF16).reshape(peers, per, width)
    store = pltpu.make_async_copy(out_v, out_ref, sems.at[9])
    store.start()
    loads[8].wait()
    q_v[...] = dotf(pair[:events], wq[...]).astype(BF16)
    store_q = pltpu.make_async_copy(q_v, q_ref, sems.at[10])
    store_q.start()
    store.wait()
    store_q.wait()


def messages(cap_e, got, code, w1, enc, b1, w2, b2, base, wq):
    peers, _, width = got.shape
    args = (got, code, w1, enc, b1, w2, b2, base, wq)
    q_shape = (enc.shape[0], width)
    tile = (peers, 8, width)
    anywhere = pl.BlockSpec(memory_space=pl.ANY)
    scratch = [pltpu.VMEM(tile, BF16)] + [pltpu.VMEM(x.shape, x.dtype) for x in args[1:]]
    scratch += [pltpu.VMEM(tile, BF16), pltpu.VMEM(q_shape, BF16), pltpu.SemaphoreType.DMA((11,))]
    return pl.pallas_call(
        functools.partial(message_kernel, cap_e),
        out_shape=(pltpu.HBM(base.shape, BF16), pltpu.HBM(q_shape, BF16)),
        in_specs=[anywhere] * len(args),
        out_specs=(anywhere, anywhere),
        scratch_shapes=scratch,
        compiler_params=pltpu.CompilerParams(vmem_limit_bytes=28 << 20),
    )(*[hbm(x) for x in args])


def prepare_kernel(to_c_ref, to_t_ref, old_ref, wh_ref, bias_ref, hits_ref, inv_ref, gh_ref):
    slots = old_ref.shape[0]
    row = to_c_ref[...].astype(F32)
    col = jnp.broadcast_to(row, (8, slots)).T[:, 0:1]
    tiles = to_t_ref[...].astype(F32)
    hits = jnp.where(jnp.logical_and(col == tiles, tiles > 0.0), 1.0, 0.0)
    counts = jnp.sum(hits, axis=1, keepdims=True)
    hits_ref[...] = hits.astype(BF16)
    inv_ref[...] = jnp.broadcast_to(jnp.maximum(counts, 1.0), inv_ref.shape)
    gh_ref[...] = (dotf(old_ref[...], wh_ref[...]) + bias_ref[1:2, :]).astype(BF16)


def prepare(to_c, to_t, old, wh, bias):
    slots = old.shape[0]
    args = (to_c, to_t, hbm(old), wh, bias)
    out = ((slots, to_t.shape[1]), BF16), ((slots, LANES), F32), ((slots, wh.shape[1]), BF16)
    return pl.pallas_call(
        prepare_kernel,
        out_shape=tuple(pltpu.HBM(*x) for x in out),
        grid=(1,),
        in_specs=[whole(x) for x in args],
        out_specs=tuple(whole(sds(*x)) for x in out),
        compiler_params=pltpu.CompilerParams(vmem_limit_bytes=24 << 20),
    )(*args)


def block_scores(qk_ref, rows, enc, slot_map, events):
    slots, width = rows.shape
    heads = qk_ref.shape[0] // events
    s = lax.dot_general(qk_ref[:, :width], rows, NT, preferred_element_type=F32)
    s = s + lax.dot_general(qk_ref[:, width:], enc, NT, preferred_element_type=F32)
    event = lax.broadcasted_iota(jnp.int32, (events, slots), 0) + 1
    bias = jnp.where(event == slot_map, 0.0, NEG)
    return s + jnp.concatenate([bias] * heads, axis=0)


def block_sums(p, rows, enc):
    slots = rows.shape[0]
    tail = jnp.concatenate([enc, jnp.ones((slots, LANES), BF16)], axis=1)
    return dotf(p, rows), dotf(p, tail)


def attend_kernel(rows_ref, enc_ref, map_ref, q_ref, w_ref, qk_ref, m_ref, a_ref):
    slots, width = rows_ref.shape
    events = q_ref.shape[0]

    @pl.when(pl.program_id(0) == 0)
    def _():
        scale = 1.4426950408889634 / HDIM**0.5
        for h in range(width // HDIM):
            cut = slice(h * HDIM, (h + 1) * HDIM)
            qk = lax.dot_general(q_ref[:, cut], w_ref[:, cut], NT, preferred_element_type=F32)
            qk_ref[h * events : (h + 1) * events, :] = (qk * scale).astype(BF16)
        m_ref[...] = jnp.full(m_ref.shape, NEG, F32)
        a_ref[...] = jnp.zeros(a_ref.shape, F32)

    rows = rows_ref[...]
    enc = enc_ref[...]
    s = block_scores(qk_ref, rows, enc, map_ref[...], events)
    m_old = m_ref[...]
    m = jnp.maximum(m_old, jnp.max(s, axis=1, keepdims=True))
    p = jnp.exp2(s - m[:, 0:1]).astype(BF16)
    scale = jnp.exp2(m_old - m)[:, 0:1]
    m_ref[...] = m
    near, far = block_sums(p, rows, enc)
    a_ref[:, :width] = scale * a_ref[:, :width] + near
    a_ref[:, width:] = scale * a_ref[:, width:] + far


def attend(rows, enc, slot_map, query, w):
    total, width = rows.shape
    block = 1024
    events = query.shape[0]
    stacked = width // HDIM * events
    shapes = (
        ((stacked, width + LANES), BF16),
        ((stacked, LANES), F32),
        ((stacked, width + 2 * LANES), F32),
    )
    return pl.pallas_call(
        attend_kernel,
        out_shape=tuple(pltpu.HBM(*x) for x in shapes),
        grid=(total // block,),
        in_specs=[
            pl.BlockSpec((block, width), lambda i: (i, 0)),
            pl.BlockSpec((block, LANES), lambda i: (i, 0)),
            pl.BlockSpec((1, block), lambda i: (0, i)),
            whole(query),
            pl.BlockSpec((w.shape[0], width), lambda i: (0, 0)),
        ],
        out_specs=tuple(whole(sds(*x)) for x in shapes),
        compiler_params=pltpu.CompilerParams(vmem_limit_bytes=28 << 20),
    )(hbm(rows), hbm(enc), hbm(slot_map), hbm(query), hbm(w))


def finish_kernel(*refs):
    ins = refs[:16]
    emb_ref, out_ref = refs[16:18]
    (got, enc, slot_map, qk, m_prev, a_prev, w, wo, hits, inv, wi, bias, gh, old, mem, to) = refs[18:34]
    tile32, near, msgs, emb_v, mem32, fresh32, out_v, sems = refs[34:]
    peers, per, width = got.shape
    slots = old.shape[0]
    cap = slots // peers
    nodes = mem.shape[0]
    parts = width // LANES
    blocks = out_v.shape[0]
    inner = w.shape[0]
    heads = width // HDIM
    events = qk.shape[0] // heads
    sources = list(ins)
    sources[6] = ins[6].at[:, pl.ds(width, width)]
    loads = starts(list(zip(sources, refs[18:34])), sems)
    loads[0].wait()
    flat = got[...].reshape(peers * per, width)
    for c in range(parts):
        tile32[c] = flat[:, c * LANES : (c + 1) * LANES].astype(F32)
    for dst, off in ((near, cap), (msgs, 0)):
        for j in range(cap):
            for c in range(parts):
                part = tile32[c, pl.ds(off + j, peers, stride=per), :]
                dst[j * peers : (j + 1) * peers, c * LANES : (c + 1) * LANES] = part.astype(BF16)
    for i in range(1, 4):
        loads[i].wait()
    s = block_scores(qk, near[...], enc[...], slot_map[...], events)
    m_new = jnp.max(s, axis=1, keepdims=True)
    p = jnp.exp2(s - m_new).astype(BF16)
    rows_sum, tail_sum = block_sums(p, near[...], enc[...])
    loads[4].wait()
    loads[5].wait()
    before = m_prev[:, 0:1]
    m = jnp.maximum(m_new, before)
    f_new = jnp.exp2(m_new - m)
    f_old = jnp.exp2(before - m)
    part_a = f_new * rows_sum + f_old * a_prev[:, :width]
    part_b = f_new * tail_sum + f_old * a_prev[:, width:]
    total = part_b[:, LANES : LANES + 1]
    mixed_a = (part_a / total).astype(BF16)
    mixed_b = (part_b[:, :LANES] / total).astype(BF16)
    loads[6].wait()
    loads[7].wait()
    outs = []
    for h in range(heads):
        cut = slice(h * HDIM, (h + 1) * HDIM)
        at = slice(h * events, (h + 1) * events)
        value = dotf(mixed_a[at], w[:width, cut]) + dotf(mixed_b[at], w[width:, cut])
        outs.append(value.astype(BF16))
    emb_v[...] = dotf(jnp.concatenate(outs, axis=1), wo[...]).astype(BF16)
    copies = [pltpu.make_async_copy(emb_v, emb_ref, sems.at[16])]
    copies[0].start()

    for i in range(8, 12):
        loads[i].wait()
    sums = dotf(hits[...], msgs[...])
    mean = (sums / inv[:, 0:1]).astype(BF16)
    gi = dotf(mean, wi[...]) + bias[0:1, :]
    loads[12].wait()
    loads[13].wait()
    r = jax.nn.sigmoid(gi[:, :width] + gh[:, :width].astype(F32))
    z = jax.nn.sigmoid(gi[:, width : 2 * width] + gh[:, width : 2 * width].astype(F32))
    c = jnp.tanh(gi[:, 2 * width :] + r * gh[:, 2 * width :].astype(F32))
    fresh = (1.0 - z) * c + z * old[...].astype(F32)
    for k in range(parts):
        fresh32[pl.ds(k, slots, stride=parts), :] = fresh[:, k * LANES : (k + 1) * LANES]
    loads[14].wait()
    spread(mem, mem32, parts)
    loads[15].wait()

    def step(i, carry):
        for k in range(16):
            s = i * 16 + k
            at = pl.multiple_of(to[s], parts)
            mem32[pl.ds(at, parts), :] = fresh32[pl.ds(pl.multiple_of(s * parts, parts), parts), :]
        return carry

    lax.fori_loop(0, slots // 16, step, 0)
    size = nodes // blocks
    for b in range(blocks):

        def back(i, carry):
            row = pl.multiple_of(i * 128, 128)
            gather_back(mem32, parts + (b * size + row) * parts, out_v.at[b], row, 128)
            return carry

        lax.fori_loop(0, size // 128, back, 0)
        copy = pltpu.make_async_copy(out_v.at[b], out_ref.at[pl.ds(b * size, size)], sems.at[17 + b])
        copy.start()
        copies.append(copy)
    for copy in copies:
        copy.wait()


def finish(got, enc, slot_map, qk, m, a, w, wo, hits, inv, wi, bias, gh, old, memory, to, blocks=4):
    args = (got, enc, slot_map, qk, m, a, w, wo, hits, inv, wi, bias, gh, old, memory, to)
    peers, per, width = got.shape
    nodes = memory.shape[0]
    slots = old.shape[0]
    parts = width // LANES
    emb_shape = (qk.shape[0] // (width // HDIM), width)
    anywhere = pl.BlockSpec(memory_space=pl.ANY)
    shapes = [x.shape for x in args[:-1]]
    shapes[6] = (w.shape[0], width)
    scratch = [pltpu.VMEM(shape, x.dtype) for shape, x in zip(shapes, args)]
    scratch += [
        pltpu.SMEM(to.shape, jnp.int32),
        pltpu.VMEM((parts, peers * per, LANES), F32),
        pltpu.VMEM((slots, width), BF16),
        pltpu.VMEM((slots, width), BF16),
        pltpu.VMEM(emb_shape, BF16),
        pltpu.VMEM(((nodes + 1) * parts, LANES), F32),
        pltpu.VMEM((slots * parts, LANES), F32),
        pltpu.VMEM((blocks, nodes // blocks, width), BF16),
        pltpu.SemaphoreType.DMA((17 + blocks,)),
    ]
    return pl.pallas_call(
        finish_kernel,
        out_shape=(pltpu.HBM(emb_shape, BF16), pltpu.HBM(memory.shape, BF16)),
        in_specs=[anywhere] * len(args),
        out_specs=(anywhere, anywhere),
        scratch_shapes=scratch,
        compiler_params=pltpu.CompilerParams(vmem_limit_bytes=44 << 20),
    )(*[hbm(x) for x in args])


def encode(dt, freq, phase):
    return jnp.cos(dt[..., None] * freq + phase).astype(BF16)


def on_device(
    memory,
    event_nodes,
    event_ticks,
    neighbour_ids,
    neighbour_ticks,
    freq,
    phase,
    w_msg1,
    b_msg1,
    w_msg2,
    b_msg2,
    w_query,
    w_keyval,
    w_out,
    gru_input,
    gru_hidden,
    gru_bias,
):
    owners = lax.axis_size(AXES)
    nodes, width = memory.shape
    events, fanout = neighbour_ids.shape
    cap_e = 4 * events // owners
    cap_n = 2 * fanout * events // owners
    rows = cap_n + 8
    shift = nodes.bit_length() - 1
    assert nodes == 1 << shift and cap_e == 4 and cap_n == 40
    table = (owners, LANES)
    req, owner_map, dt = call(
        functools.partial(place_kernel, shift, width // LANES, cap_n, rows),
        (sds(table, jnp.int32), sds(table, jnp.int32), sds(table, F32)),
        hbm(neighbour_ids.T),
        hbm(neighbour_ticks.T),
        hbm(event_nodes.T),
        hbm(event_ticks.reshape(1, events)),
        mib=8,
    )
    asked = exchange(req)

    half = 8 - cap_e
    near = cap_n - half
    ev = tuple(range(cap_n, cap_n + cap_e))
    cols_a = ev + tuple(range(near))
    cols_c = tuple(range(near, near + cap_e)) + tuple(range(near, cap_n))
    take = functools.partial(pick, asked, memory)
    sent_a = take(cols_a, (True,) * cap_e + (False,) * near)
    got_a = exchange(sent_a)
    base_c = take(cols_c, (False,) * len(cols_c)).reshape(owners, -1, width)
    old = take(ev, (True,) * cap_e)

    def spaced(x):
        return jnp.concatenate([jnp.zeros((owners, cap_e), x.dtype), x], axis=1)

    def tiled(x):
        return jnp.concatenate([x, jnp.zeros((owners, half), x.dtype)], axis=1).reshape(1, -1)

    code = tiled(owner_map[:, cap_n : cap_n + cap_e])
    map_a = spaced(owner_map[:, :near]).reshape(1, -1)
    map_c = owner_map[:, near:cap_n].T.reshape(1, -1)
    to = asked[:, cap_n : cap_n + cap_e]
    to_s = to.reshape(-1)
    hits, counts, gh = prepare(to.reshape(1, -1), to.T.reshape(1, -1), old, gru_hidden, gru_bias)
    enc_a = encode(spaced(dt[:, :near]), freq, phase).reshape(-1, LANES)
    enc_c = encode(dt[:, near:cap_n].T, freq, phase).reshape(-1, LANES)
    enc = encode(event_ticks.astype(F32), freq, phase)
    got_a, enc_a, enc_c, map_a, map_c, hits, counts, gh, base_c, to_s = lax.optimization_barrier(
        (got_a, enc_a, enc_c, map_a, map_c, hits, counts, gh, base_c, to_s)
    )
    sent_c, query = messages(
        cap_e,
        got_a.reshape(owners, -1, width),
        code,
        w_msg1,
        enc,
        b_msg1.reshape(1, -1),
        w_msg2,
        b_msg2.reshape(1, -1),
        base_c,
        w_query,
    )
    got_c = exchange(sent_c)
    qk, m, a = attend(got_a, enc_a, map_a, query, w_keyval)
    return finish(
        got_c,
        enc_c,
        map_c,
        qk,
        m,
        a,
        w_keyval,
        w_out,
        hits,
        counts,
        gru_input,
        gru_bias,
        gh,
        old,
        memory,
        to_s,
    )


def solution(mesh):
    split = P(AXES, None)
    in_specs = (split, split, P(AXES), split, split) + (P(),) * 12
    return jax.shard_map(
        on_device, mesh=mesh, in_specs=in_specs, out_specs=(split, split), check_vma=False
    )
```

```python
import functools

import jax
import jax.numpy as jnp
from jax import lax
from jax.experimental import pallas as pl
from jax.experimental.pallas import tpu as pltpu
from jax.sharding import PartitionSpec as P

HDIM = 128
LANES = 128
PIECES = 4
AXES = ("grp", "dev")
F32 = jnp.float32
BF16 = jnp.bfloat16
NEG = -1e30
NT = (((1,), (1,)), ((), ()))


def dotf(a, b):
    return jnp.dot(a, b, preferred_element_type=F32)


def exchange(x):
    return lax.all_to_all(x, AXES, split_axis=0, concat_axis=0, tiled=True)


def call(kernel, out_shape, *args, scalars=0, scratch=(), mib=16):
    return pl.pallas_call(
        kernel,
        out_shape=out_shape,
        grid_spec=pltpu.PrefetchScalarGridSpec(
            num_scalar_prefetch=scalars,
            grid=(),
            in_specs=[pl.BlockSpec(memory_space=pltpu.VMEM)] * (len(args) - scalars),
            out_specs=jax.tree.map(lambda _: pl.BlockSpec(memory_space=pltpu.VMEM), out_shape),
            scratch_shapes=scratch,
        ),
        compiler_params=pltpu.CompilerParams(vmem_limit_bytes=mib << 20),
    )(*args)


def hbm(x):
    return pltpu.with_memory_space_constraint(x, pltpu.HBM)


def vmem(x):
    return pltpu.with_memory_space_constraint(x, pltpu.VMEM)


def whole(x):
    zeros = (0,) * x.ndim
    return pl.BlockSpec(x.shape, lambda *_: zeros)


def sds(shape, dtype):
    return jax.ShapeDtypeStruct(shape, dtype)


def place_kernel(shift, parts, cap_n, rows, nid_ref, nt_ref, en_ref, tick_ref, req_ref, map_ref, dt_ref):
    fanout, events = nid_ref.shape
    owners = req_ref.shape[0]
    i0 = lax.broadcasted_iota(jnp.int32, (owners, events), 0)
    e0 = lax.broadcasted_iota(jnp.int32, (events, events), 0)
    e1 = lax.broadcasted_iota(jnp.int32, (events, events), 1)
    tri = jnp.where(e0 <= e1, 1.0, 0.0)
    both = jnp.concatenate([tri, jnp.ones((events, events), F32)], axis=1).astype(BF16)
    srow = lax.broadcasted_iota(jnp.int32, (rows, events), 0)
    lane = lax.broadcasted_iota(jnp.int32, (1, events), 1)
    tick = tick_ref[...]
    mask = (1 << shift) - 1
    acc = jnp.zeros((6 * rows, owners), F32)
    base = jnp.zeros((owners, events), F32)
    zero = jnp.zeros((1, events), jnp.int32)
    held = []
    for k in range(fanout + 2):
        near = k < fanout
        if k == fanout:
            base = jnp.zeros((owners, events), F32)
        ids = nid_ref[k : k + 1, :] if near else en_ref[k - fanout : k - fanout + 1, :]
        local = jnp.bitwise_and(ids, mask)
        hit = i0 == jnp.right_shift(ids, shift)
        onehot = jnp.where(hit, 1.0, 0.0)
        ohb = onehot.astype(BF16)
        ranks = dotf(ohb, both)
        cum = ranks[:, :events] + base
        base = base + ranks[:, events:]
        slot = jnp.sum(onehot * cum, axis=0, keepdims=True).astype(jnp.int32) - 1
        if near:
            d = tick - nt_ref[k : k + 1, :] + 131072
            code = lane + 1
            digits = (d & 255, jnp.right_shift(d, 8) & 255, jnp.right_shift(d, 16))
            value = (local + 1) * parts
        else:
            slot = slot + cap_n
            code = lane + (1 + events * (k - fanout))
            digits = (zero, zero, zero)
            value = (local + 1) * parts
        vals = (value & 255, jnp.right_shift(value, 8), code) + digits
        so = srow == slot
        table = jnp.concatenate([jnp.where(so, v.astype(F32), 0.0) for v in vals], axis=0)
        held.append((table.astype(BF16), ohb))
        if len(held) == 2:
            lhs = jnp.concatenate([x[0] for x in held], axis=1)
            rhs = jnp.concatenate([x[1] for x in held], axis=1)
            acc = acc + lax.dot_general(lhs, rhs, NT, preferred_element_type=F32)
            held = []
    a = [acc[i * rows : (i + 1) * rows] for i in range(6)]
    pad = jnp.zeros((LANES - rows, owners), F32)

    def turned(x):
        return jnp.concatenate([x, pad], axis=0).T

    req_ref[...] = turned(a[0] + 256.0 * a[1]).astype(jnp.int32)
    map_ref[...] = turned(a[2]).astype(jnp.int32)
    dt = a[3] + 256.0 * a[4] + 65536.0 * a[5] - 131072.0
    dt_ref[...] = turned(jnp.where(a[2] > 0.0, dt, 0.0))


def spread(src_ref, dst_ref, base=0):
    rows, width = src_ref.shape
    parts = width // LANES
    block = 128

    def step(i, carry):
        r = pl.multiple_of(i * block, block)
        for c in range(parts):
            part = src_ref[pl.ds(r, block), c * LANES : (c + 1) * LANES].astype(F32)
            dst_ref[pl.ds(base + r * parts + c, block, stride=parts), :] = part
        return carry

    lax.fori_loop(0, rows // block, step, 0)


def gather_back(src_ref, base, dst_ref, row, rows):
    parts = dst_ref.shape[1] // LANES
    for c in range(parts):
        part = src_ref[pl.ds(base + c, rows, stride=parts), :]
        dst_ref[pl.ds(row, rows), c * LANES : (c + 1) * LANES] = part.astype(dst_ref.dtype)


def pick_group(n):
    return 16 // n if n < 16 else 2


def pick_kernel(cols, static, req_ref, mem_ref, out_ref, req_s, mem_v, mem32, stage, out_v, sems):
    peers = req_ref.shape[0]
    width = mem_ref.shape[1]
    parts = width // LANES
    n = len(cols)
    blocks = out_v.shape[0]
    group = pick_group(n)
    total = n * group
    steps = peers // group // blocks
    load_req = pltpu.make_async_copy(req_ref, req_s, sems.at[0])
    load_req.start()
    loads = []
    piece = mem_ref.shape[0] // PIECES
    for i in range(PIECES):
        at = pl.ds(i * piece, piece)
        loads.append(pltpu.make_async_copy(mem_ref.at[at], mem_v.at[at], sems.at[1 + i]))
        loads[i].start()
    mem32[0:parts, :] = jnp.zeros((parts, LANES), F32)
    for i in range(PIECES):
        loads[i].wait()
        spread(mem_v.at[pl.ds(i * piece, piece)], mem32, parts + i * piece * parts)
    load_req.wait()
    copies = []
    for b in range(blocks):

        def step(i):
            for g in range(group):
                o = (b * steps + i) * group + g
                for j, col in enumerate(cols):
                    at = pl.multiple_of(req_s[o, col], parts)
                    s = (g * n + j) * parts
                    stage[s : s + parts, :] = mem32[pl.ds(at, parts), :]
            r = i * total if static else pl.multiple_of(i * total, total)
            gather_back(stage, 0, out_v.at[b], r, total)

        if static:
            for i in range(steps):
                step(i)
        else:
            lax.fori_loop(0, steps, lambda i, carry: (step(i), carry)[1], 0)
        size = steps * total
        copy = pltpu.make_async_copy(out_v.at[b], out_ref.at[pl.ds(b * size, size)], sems.at[1 + PIECES + b])
        copy.start()
        copies.append(copy)
    for copy in copies:
        copy.wait()


def pick(req, memory, cols, static=False, blocks=4):
    peers = req.shape[0]
    nodes, width = memory.shape
    parts = width // LANES
    rows = peers * len(cols)
    anywhere = pl.BlockSpec(memory_space=pl.ANY)
    return pl.pallas_call(
        functools.partial(pick_kernel, cols, static),
        out_shape=pltpu.HBM((rows, width), BF16),
        in_specs=[anywhere, anywhere],
        out_specs=anywhere,
        scratch_shapes=[
            pltpu.SMEM(req.shape, jnp.int32),
            pltpu.VMEM((nodes, width), BF16),
            pltpu.VMEM(((nodes + 1) * parts, LANES), F32),
            pltpu.VMEM((len(cols) * pick_group(len(cols)) * parts, LANES), F32),
            pltpu.VMEM((blocks, rows // blocks, width), BF16),
            pltpu.SemaphoreType.DMA((1 + PIECES + blocks,)),
        ],
        compiler_params=pltpu.CompilerParams(vmem_limit_bytes=16 << 20),
    )(hbm(req), hbm(memory))


def starts(pairs, sems):
    copies = [pltpu.make_async_copy(src, dst, sems.at[i]) for i, (src, dst) in enumerate(pairs)]
    for copy in copies:
        copy.start()
    return copies


def message_kernel(cap_e, *refs):
    ins = refs[:9]
    out_ref, q_ref = refs[9:11]
    rows, code, w1, enc, b1, w2, b2, base, wq, back, hidden, out_v, q_v, sems = refs[11:]
    peers, per, width = rows.shape
    slots = peers * per
    events = enc.shape[0]
    sources = (ins[0].at[:, 0:per, :],) + tuple(ins[1:])
    loads = starts(list(zip(sources, (rows, code, w1, enc, b1, w2, b2, base, wq))), sems)
    loads[1].wait()
    target = lax.broadcasted_iota(jnp.int32, (2 * events, slots), 0) + 1
    sel = jnp.where(target == code[...], 1.0, 0.0)
    back[...] = sel.T.astype(BF16)
    loads[0].wait()
    pair = dotf(sel.astype(BF16), rows[...].reshape(slots, width)).astype(BF16)
    for i in (2, 3, 4):
        loads[i].wait()
    block = 256
    for i in range(hidden.shape[1] // block):
        cut = slice(i * block, (i + 1) * block)
        second = dotf(pair, w1[width : 2 * width, cut])
        third = dotf(enc[...], w1[2 * width :, cut]) + b1[:, cut]
        both = jnp.concatenate([second[events:] + third, second[:events] + third], axis=0)
        hidden[:, cut] = jnp.maximum(dotf(pair, w1[:width, cut]) + both, 0.0).astype(BF16)
    for i in (5, 6):
        loads[i].wait()
    msg = (dotf(hidden[...], w2[...]) + b2[...]).astype(BF16)
    j = lax.broadcasted_iota(jnp.int32, (block, width), 0) & (per - 1)
    loads[7].wait()
    stores = []
    for i in range(slots // block):
        cut = slice(i * block // per, (i + 1) * block // per)
        placed = dotf(back[i * block : (i + 1) * block, :], msg)
        kept = base[cut].reshape(block, width).astype(F32)
        out_v[cut] = jnp.where(j < cap_e, placed, kept).astype(BF16).reshape(block // per, per, width)
        stores.append(pltpu.make_async_copy(out_v.at[cut], out_ref.at[cut], sems.at[9 + i]))
        stores[i].start()
    loads[8].wait()
    q_v[...] = dotf(pair[:events], wq[...]).astype(BF16)
    stores.append(pltpu.make_async_copy(q_v, q_ref, sems.at[8]))
    stores[-1].start()
    for store in stores:
        store.wait()


def messages(cap_e, got, code, w1, enc, b1, w2, b2, base, wq):
    peers, _, width = got.shape
    args = (got, code, w1, enc, b1, w2, b2, base, wq)
    q_shape = (enc.shape[0], width)
    tile = (peers, 8, width)
    anywhere = pl.BlockSpec(memory_space=pl.ANY)
    scratch = [pltpu.VMEM(tile, BF16)] + [pltpu.VMEM(x.shape, x.dtype) for x in args[1:]]
    scratch += [
        pltpu.VMEM((peers * 8, 2 * q_shape[0]), BF16),
        pltpu.VMEM((2 * q_shape[0], w1.shape[1]), BF16),
        pltpu.VMEM(tile, BF16),
        pltpu.VMEM(q_shape, BF16),
        pltpu.SemaphoreType.DMA((9 + peers * 8 // 256,)),
    ]
    return pl.pallas_call(
        functools.partial(message_kernel, cap_e),
        out_shape=(pltpu.HBM(base.shape, BF16), pltpu.HBM(q_shape, BF16)),
        in_specs=[anywhere] * len(args),
        out_specs=(anywhere, anywhere),
        scratch_shapes=scratch,
        compiler_params=pltpu.CompilerParams(vmem_limit_bytes=28 << 20),
    )(*[hbm(x) for x in args])


def prepare_kernel(to_c_ref, to_t_ref, old_ref, wh_ref, bias_ref, hits_ref, inv_ref, gh_ref):
    slots = old_ref.shape[0]
    row = to_c_ref[...].astype(F32)
    col = jnp.broadcast_to(row, (8, slots)).T[:, 0:1]
    tiles = to_t_ref[...].astype(F32)
    hits = jnp.where(jnp.logical_and(col == tiles, tiles > 0.0), 1.0, 0.0)
    counts = jnp.sum(hits, axis=1, keepdims=True)
    hits_ref[...] = hits.astype(BF16)
    inv_ref[...] = jnp.broadcast_to(1.0 / jnp.maximum(counts, 1.0), inv_ref.shape)
    gh_ref[...] = (dotf(old_ref[...], wh_ref[...]) + bias_ref[1:2, :]).astype(BF16)


def prepare(to_c, to_t, old, wh, bias):
    slots = old.shape[0]
    args = (to_c, to_t, hbm(old), wh, bias)
    out = ((slots, to_t.shape[1]), BF16), ((slots, LANES), F32), ((slots, wh.shape[1]), BF16)
    return pl.pallas_call(
        prepare_kernel,
        out_shape=tuple(pltpu.HBM(*x) for x in out),
        grid=(1,),
        in_specs=[whole(x) for x in args],
        out_specs=tuple(whole(sds(*x)) for x in out),
        compiler_params=pltpu.CompilerParams(vmem_limit_bytes=24 << 20),
    )(*args)


def block_scores(qk_ref, rows, enc, slot_map, events):
    slots, width = rows.shape
    heads = qk_ref.shape[0] // events
    s = lax.dot_general(qk_ref[:, :width], rows, NT, preferred_element_type=F32)
    s = s + lax.dot_general(qk_ref[:, width:], enc, NT, preferred_element_type=F32)
    event = lax.broadcasted_iota(jnp.int32, (events, slots), 0) + 1
    bias = jnp.where(event == slot_map, 0.0, NEG)
    return s + jnp.concatenate([bias] * heads, axis=0)


def block_sums(p, rows, enc):
    slots = rows.shape[0]
    tail = jnp.concatenate([enc, jnp.ones((slots, LANES), BF16)], axis=1)
    return dotf(p, rows), dotf(p, tail)


def attend_kernel(rows_ref, enc_ref, map_ref, q_ref, w_ref, qk_ref, m_ref, a_ref):
    slots, width = rows_ref.shape
    events = q_ref.shape[0]

    @pl.when(pl.program_id(0) == 0)
    def _():
        scale = 1.4426950408889634 / HDIM**0.5
        for h in range(width // HDIM):
            cut = slice(h * HDIM, (h + 1) * HDIM)
            qk = lax.dot_general(q_ref[:, cut], w_ref[:, cut], NT, preferred_element_type=F32)
            qk_ref[h * events : (h + 1) * events, :] = (qk * scale).astype(BF16)
        m_ref[...] = jnp.full(m_ref.shape, NEG, F32)
        a_ref[...] = jnp.zeros(a_ref.shape, F32)

    rows = rows_ref[...]
    enc = enc_ref[...]
    s = block_scores(qk_ref, rows, enc, map_ref[...], events)
    m_old = m_ref[...]
    m = jnp.maximum(m_old, jnp.max(s, axis=1, keepdims=True))
    p = jnp.exp2(s - m[:, 0:1]).astype(BF16)
    scale = jnp.exp2(m_old - m)[:, 0:1]
    m_ref[...] = m
    near, far = block_sums(p, rows, enc)
    a_ref[:, :width] = scale * a_ref[:, :width] + near
    a_ref[:, width:] = scale * a_ref[:, width:] + far


def attend(rows, enc, slot_map, query, w):
    total, width = rows.shape
    block = 1024
    events = query.shape[0]
    stacked = width // HDIM * events
    shapes = (
        ((stacked, width + LANES), BF16),
        ((stacked, LANES), F32),
        ((stacked, width + 2 * LANES), F32),
    )
    return pl.pallas_call(
        attend_kernel,
        out_shape=tuple(pltpu.HBM(*x) for x in shapes),
        grid=(total // block,),
        in_specs=[
            pl.BlockSpec((block, width), lambda i: (i, 0)),
            pl.BlockSpec((block, LANES), lambda i: (i, 0)),
            pl.BlockSpec((1, block), lambda i: (0, i)),
            whole(query),
            pl.BlockSpec((w.shape[0], width), lambda i: (0, 0)),
        ],
        out_specs=tuple(whole(sds(*x)) for x in shapes),
        compiler_params=pltpu.CompilerParams(vmem_limit_bytes=28 << 20),
    )(hbm(rows), hbm(enc), hbm(slot_map), hbm(query), hbm(w))


def sigmoid(x):
    return 0.5 * jnp.tanh(0.5 * x) + 0.5


def finish_kernel(*refs):
    got = refs[0]
    ins = refs[1:16]
    emb_ref, out_ref = refs[16:18]
    (enc, slot_map, qk, hits, inv, wi, bias, gh, old, m_prev, a_prev, w, wo, mem, to) = refs[18:33]
    tile32, near, msgs, gates, emb_v, mem32, fresh32, out_v, sems = refs[33:]
    peers, per, width = got.shape
    slots = old.shape[0]
    cap = slots // peers
    nodes = mem.shape[0]
    parts = width // LANES
    blocks = out_v.shape[0]
    heads = width // HDIM
    events = qk.shape[0] // heads
    sources = list(ins)
    sources[11] = ins[11].at[:, pl.ds(width, width)]
    loads = starts(list(zip(sources, refs[18:33])), sems)
    flat = got[...].reshape(peers * per, width)
    for c in range(parts):
        tile32[c] = flat[:, c * LANES : (c + 1) * LANES].astype(F32)
    for dst, off in ((near, cap), (msgs, 0)):
        for j in range(cap):
            for c in range(parts):
                part = tile32[c, pl.ds(off + j, peers, stride=per), :]
                dst[j * peers : (j + 1) * peers, c * LANES : (c + 1) * LANES] = part.astype(BF16)
    for i in range(5):
        loads[i].wait()
    s = block_scores(qk, near[...], enc[...], slot_map[...], events)
    sums = dotf(hits[...], msgs[...])
    m_new = jnp.max(s, axis=1, keepdims=True)
    p = jnp.exp2(s - m_new).astype(BF16)
    mean = (sums * inv[:, 0:1]).astype(BF16)
    for i in (5, 6):
        loads[i].wait()
    gates[...] = dotf(mean, wi[...]) + bias[0:1, :]
    rows_sum, tail_sum = block_sums(p, near[...], enc[...])
    for i in (7, 8):
        loads[i].wait()
    block = 128
    for i in range(slots // block):
        at = slice(i * block, (i + 1) * block)
        r = sigmoid(gates[at, :width] + gh[at, :width].astype(F32))
        z = sigmoid(gates[at, width : 2 * width] + gh[at, width : 2 * width].astype(F32))
        c = jnp.tanh(gates[at, 2 * width :] + r * gh[at, 2 * width :].astype(F32))
        fresh = (1.0 - z) * c + z * old[at, :].astype(F32)
        for k in range(parts):
            cut = slice(k * LANES, (k + 1) * LANES)
            fresh32[pl.ds(i * block * parts + k, block, stride=parts), :] = fresh[:, cut]
    for i in (9, 10, 11, 12):
        loads[i].wait()
    before = m_prev[:, 0:1]
    m = jnp.maximum(m_new, before)
    f_new = jnp.exp2(m_new - m)
    f_old = jnp.exp2(before - m)
    ones_at = width + LANES
    total = f_new * tail_sum[:, LANES : LANES + 1] + f_old * a_prev[:, ones_at : ones_at + 1]
    f_new = f_new / total
    f_old = f_old / total
    mixed_a = (f_new * rows_sum + f_old * a_prev[:, :width]).astype(BF16)
    mixed_b = (f_new * tail_sum[:, :LANES] + f_old * a_prev[:, width:ones_at]).astype(BF16)
    outs = []
    for h in range(heads):
        cut = slice(h * HDIM, (h + 1) * HDIM)
        at = slice(h * events, (h + 1) * events)
        value = dotf(mixed_a[at], w[:width, cut]) + dotf(mixed_b[at], w[width:, cut])
        outs.append(value.astype(BF16))
    emb_v[...] = dotf(jnp.concatenate(outs, axis=1), wo[...]).astype(BF16)
    copies = [pltpu.make_async_copy(emb_v, emb_ref, sems.at[15])]
    copies[0].start()
    loads[13].wait()
    spread(mem, mem32, parts)
    loads[14].wait()

    def step(i, carry):
        for k in range(16):
            s = i * 16 + k
            at = pl.multiple_of(to[s], parts)
            mem32[pl.ds(at, parts), :] = fresh32[pl.ds(pl.multiple_of(s * parts, parts), parts), :]
        return carry

    lax.fori_loop(0, slots // 16, step, 0)
    size = nodes // blocks
    for b in range(blocks):

        def back(i, carry):
            row = pl.multiple_of(i * 128, 128)
            gather_back(mem32, parts + (b * size + row) * parts, out_v.at[b], row, 128)
            return carry

        lax.fori_loop(0, size // 128, back, 0)
        copy = pltpu.make_async_copy(out_v.at[b], out_ref.at[pl.ds(b * size, size)], sems.at[16 + b])
        copy.start()
        copies.append(copy)
    for copy in copies:
        copy.wait()


def finish(got, enc, slot_map, qk, hits, inv, wi, bias, gh, old, m, a, w, wo, memory, to, blocks=4):
    args = (enc, slot_map, qk, hits, inv, wi, bias, gh, old, m, a, w, wo, memory, to)
    peers, per, width = got.shape
    nodes = memory.shape[0]
    slots = old.shape[0]
    parts = width // LANES
    emb_shape = (qk.shape[0] // (width // HDIM), width)
    anywhere = pl.BlockSpec(memory_space=pl.ANY)
    shapes = [x.shape for x in args[:-1]]
    shapes[11] = (w.shape[0], width)
    scratch = [pltpu.VMEM(shape, x.dtype) for shape, x in zip(shapes, args)]
    scratch += [
        pltpu.SMEM(to.shape, jnp.int32),
        pltpu.VMEM((parts, peers * per, LANES), F32),
        pltpu.VMEM((slots, width), BF16),
        pltpu.VMEM((slots, width), BF16),
        pltpu.VMEM((slots, wi.shape[1]), F32),
        pltpu.VMEM(emb_shape, BF16),
        pltpu.VMEM(((nodes + 1) * parts, LANES), F32),
        pltpu.VMEM((slots * parts, LANES), F32),
        pltpu.VMEM((blocks, nodes // blocks, width), BF16),
        pltpu.SemaphoreType.DMA((16 + blocks,)),
    ]
    return pl.pallas_call(
        finish_kernel,
        out_shape=(pltpu.HBM(emb_shape, BF16), pltpu.HBM(memory.shape, BF16)),
        in_specs=[pl.BlockSpec(memory_space=pltpu.VMEM)] + [anywhere] * len(args),
        out_specs=(anywhere, anywhere),
        scratch_shapes=scratch,
        compiler_params=pltpu.CompilerParams(vmem_limit_bytes=44 << 20),
    )(got, *[hbm(x) for x in args])


def encode(dt, freq, phase):
    return jnp.cos(dt[..., None] * freq + phase).astype(BF16)


def on_device(
    memory,
    event_nodes,
    event_ticks,
    neighbour_ids,
    neighbour_ticks,
    freq,
    phase,
    w_msg1,
    b_msg1,
    w_msg2,
    b_msg2,
    w_query,
    w_keyval,
    w_out,
    gru_input,
    gru_hidden,
    gru_bias,
):
    owners = lax.axis_size(AXES)
    nodes, width = memory.shape
    events, fanout = neighbour_ids.shape
    cap_e = 4 * events // owners
    cap_n = 2 * fanout * events // owners
    rows = cap_n + 8
    shift = nodes.bit_length() - 1
    assert nodes == 1 << shift and cap_e == 4 and cap_n == 40
    table = (owners, LANES)
    req, owner_map, dt = call(
        functools.partial(place_kernel, shift, width // LANES, cap_n, rows),
        (sds(table, jnp.int32), sds(table, jnp.int32), sds(table, F32)),
        hbm(neighbour_ids.T),
        hbm(neighbour_ticks.T),
        hbm(event_nodes.T),
        hbm(event_ticks.reshape(1, events)),
        mib=8,
    )
    asked = exchange(req)

    half = 8 - cap_e
    near = cap_n - half
    ev = tuple(range(cap_n, cap_n + cap_e))
    cols_a = ev + tuple(range(near))
    cols_c = tuple(range(near, near + cap_e)) + tuple(range(near, cap_n))
    take = functools.partial(pick, asked, memory)
    sent_a = take(cols_a, static=True, blocks=8)
    got_a = exchange(sent_a)
    base_c = take(cols_c).reshape(owners, -1, width)
    old = take(ev)

    def spaced(x):
        return jnp.concatenate([jnp.zeros((owners, cap_e), x.dtype), x], axis=1)

    def tiled(x):
        return jnp.concatenate([x, jnp.zeros((owners, half), x.dtype)], axis=1).reshape(1, -1)

    code = tiled(owner_map[:, cap_n : cap_n + cap_e])
    map_a = spaced(owner_map[:, :near]).reshape(1, -1)
    map_c = owner_map[:, near:cap_n].T.reshape(1, -1)
    to = asked[:, cap_n : cap_n + cap_e]
    to_s = to.reshape(-1)
    hits, inv, gh = prepare(to.reshape(1, -1), to.T.reshape(1, -1), old, gru_hidden, gru_bias)
    enc_a = encode(spaced(dt[:, :near]), freq, phase).reshape(-1, LANES)
    enc_c = encode(dt[:, near:cap_n].T, freq, phase).reshape(-1, LANES)
    enc = encode(event_ticks.astype(F32), freq, phase)
    got_a, enc_a, enc_c, map_a, map_c, hits, inv, gh, base_c, to_s = lax.optimization_barrier(
        (got_a, enc_a, enc_c, map_a, map_c, hits, inv, gh, base_c, to_s)
    )
    sent_c, query = messages(
        cap_e,
        got_a.reshape(owners, -1, width),
        code,
        w_msg1,
        enc,
        b_msg1.reshape(1, -1),
        w_msg2,
        b_msg2.reshape(1, -1),
        base_c,
        w_query,
    )
    got_c = exchange(sent_c)
    qk, m, a = attend(got_a, enc_a, map_a, query, w_keyval)
    return finish(
        got_c,
        enc_c,
        map_c,
        qk,
        hits,
        inv,
        gru_input,
        gru_bias,
        gh,
        old,
        m,
        a,
        w_keyval,
        w_out,
        memory,
        to_s,
    )


def solution(mesh):
    split = P(AXES, None)
    in_specs = (split, split, P(AXES), split, split) + (P(),) * 12
    return jax.shard_map(
        on_device, mesh=mesh, in_specs=in_specs, out_specs=(split, split), check_vma=False
    )
```

```python
import functools

import jax
import jax.numpy as jnp
from jax import lax
from jax.experimental import pallas as pl
from jax.experimental.pallas import tpu as pltpu
from jax.sharding import PartitionSpec as P

HDIM = 128
LANES = 128
PIECES = 4
AXES = ("grp", "dev")
F32 = jnp.float32
BF16 = jnp.bfloat16
NEG = -1e30
NT = (((1,), (1,)), ((), ()))


def dotf(a, b):
    return jnp.dot(a, b, preferred_element_type=F32)


def exchange(x):
    return lax.all_to_all(x, AXES, split_axis=0, concat_axis=0, tiled=True)


def call(kernel, out_shape, *args, scalars=0, scratch=(), mib=16):
    return pl.pallas_call(
        kernel,
        out_shape=out_shape,
        grid_spec=pltpu.PrefetchScalarGridSpec(
            num_scalar_prefetch=scalars,
            grid=(),
            in_specs=[pl.BlockSpec(memory_space=pltpu.VMEM)] * (len(args) - scalars),
            out_specs=jax.tree.map(lambda _: pl.BlockSpec(memory_space=pltpu.VMEM), out_shape),
            scratch_shapes=scratch,
        ),
        compiler_params=pltpu.CompilerParams(vmem_limit_bytes=mib << 20),
    )(*args)


def hbm(x):
    return pltpu.with_memory_space_constraint(x, pltpu.HBM)


def vmem(x):
    return pltpu.with_memory_space_constraint(x, pltpu.VMEM)


def whole(x):
    zeros = (0,) * x.ndim
    return pl.BlockSpec(x.shape, lambda *_: zeros)


def sds(shape, dtype):
    return jax.ShapeDtypeStruct(shape, dtype)


def place_kernel(shift, parts, cap_n, rows, nid_ref, nt_ref, en_ref, tick_ref, req_ref, map_ref, dt_ref):
    fanout, events = nid_ref.shape
    owners = req_ref.shape[0]
    i0 = lax.broadcasted_iota(jnp.int32, (owners, events), 0)
    e0 = lax.broadcasted_iota(jnp.int32, (events, events), 0)
    e1 = lax.broadcasted_iota(jnp.int32, (events, events), 1)
    tri = jnp.where(e0 <= e1, 1.0, 0.0)
    both = jnp.concatenate([tri, jnp.ones((events, events), F32)], axis=1).astype(BF16)
    srow = lax.broadcasted_iota(jnp.int32, (rows, events), 0)
    lane = lax.broadcasted_iota(jnp.int32, (1, events), 1)
    tick = tick_ref[...]
    mask = (1 << shift) - 1
    acc = jnp.zeros((6 * rows, owners), F32)
    base = jnp.zeros((owners, events), F32)
    zero = jnp.zeros((1, events), jnp.int32)
    held = []
    for k in range(fanout + 2):
        near = k < fanout
        if k == fanout:
            base = jnp.zeros((owners, events), F32)
        ids = nid_ref[k : k + 1, :] if near else en_ref[k - fanout : k - fanout + 1, :]
        local = jnp.bitwise_and(ids, mask)
        hit = i0 == jnp.right_shift(ids, shift)
        onehot = jnp.where(hit, 1.0, 0.0)
        ohb = onehot.astype(BF16)
        ranks = dotf(ohb, both)
        cum = ranks[:, :events] + base
        base = base + ranks[:, events:]
        slot = jnp.sum(onehot * cum, axis=0, keepdims=True).astype(jnp.int32) - 1
        if near:
            d = tick - nt_ref[k : k + 1, :] + 131072
            code = lane + 1
            digits = (d & 255, jnp.right_shift(d, 8) & 255, jnp.right_shift(d, 16))
            value = (local + 1) * parts
        else:
            slot = slot + cap_n
            code = lane + (1 + events * (k - fanout))
            digits = (zero, zero, zero)
            value = (local + 1) * parts
        vals = (value & 255, jnp.right_shift(value, 8), code) + digits
        so = srow == slot
        table = jnp.concatenate([jnp.where(so, v.astype(F32), 0.0) for v in vals], axis=0)
        held.append((table.astype(BF16), ohb))
        if len(held) == 2:
            lhs = jnp.concatenate([x[0] for x in held], axis=1)
            rhs = jnp.concatenate([x[1] for x in held], axis=1)
            acc = acc + lax.dot_general(lhs, rhs, NT, preferred_element_type=F32)
            held = []
    a = [acc[i * rows : (i + 1) * rows] for i in range(6)]
    pad = jnp.zeros((LANES - rows, owners), F32)

    def turned(x):
        return jnp.concatenate([x, pad], axis=0).T

    req_ref[...] = turned(a[0] + 256.0 * a[1]).astype(jnp.int32)
    map_ref[...] = turned(a[2]).astype(jnp.int32)
    dt = a[3] + 256.0 * a[4] + 65536.0 * a[5] - 131072.0
    dt_ref[...] = turned(jnp.where(a[2] > 0.0, dt, 0.0))


def spread(src_ref, dst_ref, base=0, static=False):
    rows, width = src_ref.shape
    parts = width // LANES
    block = 128

    def step(r):
        for c in range(parts):
            part = src_ref[pl.ds(r, block), c * LANES : (c + 1) * LANES].astype(F32)
            dst_ref[pl.ds(base + r * parts + c, block, stride=parts), :] = part

    def turn(i, carry):
        step(pl.multiple_of(i * block, block))
        return carry

    if static:
        for i in range(rows // block):
            step(i * block)
    else:
        lax.fori_loop(0, rows // block, turn, 0)


def gather_back(src_ref, base, dst_ref, row, rows):
    parts = dst_ref.shape[1] // LANES
    for c in range(parts):
        part = src_ref[pl.ds(base + c, rows, stride=parts), :]
        dst_ref[pl.ds(row, rows), c * LANES : (c + 1) * LANES] = part.astype(dst_ref.dtype)


def pick_group(n):
    return 16 // n if n < 16 else 2


def pick_kernel(cols, static, req_ref, mem_ref, out_ref, req_s, mem_v, mem32, stage, out_v, sems):
    peers = req_ref.shape[0]
    width = mem_ref.shape[1]
    parts = width // LANES
    n = len(cols)
    blocks = out_v.shape[0]
    group = pick_group(n)
    total = n * group
    steps = peers // group // blocks
    load_req = pltpu.make_async_copy(req_ref, req_s, sems.at[0])
    load_req.start()
    loads = []
    piece = mem_ref.shape[0] // PIECES
    for i in range(PIECES):
        at = pl.ds(i * piece, piece)
        loads.append(pltpu.make_async_copy(mem_ref.at[at], mem_v.at[at], sems.at[1 + i]))
        loads[i].start()
    mem32[0:parts, :] = jnp.zeros((parts, LANES), F32)
    for i in range(PIECES):
        loads[i].wait()
        spread(mem_v.at[pl.ds(i * piece, piece)], mem32, parts + i * piece * parts)
    load_req.wait()
    copies = []
    for b in range(blocks):

        def step(i):
            for g in range(group):
                o = (b * steps + i) * group + g
                for j, col in enumerate(cols):
                    at = pl.multiple_of(req_s[o, col], parts)
                    s = (g * n + j) * parts
                    stage[s : s + parts, :] = mem32[pl.ds(at, parts), :]
            r = i * total if static else pl.multiple_of(i * total, total)
            gather_back(stage, 0, out_v.at[b], r, total)

        if static:
            for i in range(steps):
                step(i)
        else:
            lax.fori_loop(0, steps, lambda i, carry: (step(i), carry)[1], 0)
        size = steps * total
        copy = pltpu.make_async_copy(out_v.at[b], out_ref.at[pl.ds(b * size, size)], sems.at[1 + PIECES + b])
        copy.start()
        copies.append(copy)
    for copy in copies:
        copy.wait()


def pick(req, memory, cols, static=False, blocks=4):
    peers = req.shape[0]
    nodes, width = memory.shape
    parts = width // LANES
    rows = peers * len(cols)
    anywhere = pl.BlockSpec(memory_space=pl.ANY)
    return pl.pallas_call(
        functools.partial(pick_kernel, cols, static),
        out_shape=pltpu.HBM((rows, width), BF16),
        in_specs=[anywhere, anywhere],
        out_specs=anywhere,
        scratch_shapes=[
            pltpu.SMEM(req.shape, jnp.int32),
            pltpu.VMEM((nodes, width), BF16),
            pltpu.VMEM(((nodes + 1) * parts, LANES), F32),
            pltpu.VMEM((len(cols) * pick_group(len(cols)) * parts, LANES), F32),
            pltpu.VMEM((blocks, rows // blocks, width), BF16),
            pltpu.SemaphoreType.DMA((1 + PIECES + blocks,)),
        ],
        compiler_params=pltpu.CompilerParams(vmem_limit_bytes=16 << 20),
    )(hbm(req), hbm(memory))


def starts(pairs, sems):
    copies = [pltpu.make_async_copy(src, dst, sems.at[i]) for i, (src, dst) in enumerate(pairs)]
    for copy in copies:
        copy.start()
    return copies


def message_kernel(cap_e, *refs):
    w1 = refs[0]
    ins = refs[1:9]
    out_ref, q_ref = refs[9:11]
    rows, code, enc, b1, w2, b2, base, wq, back, hidden, out_v, q_v, sems = refs[11:]
    peers, per, width = rows.shape
    slots = peers * per
    events = enc.shape[0]
    sources = (ins[0].at[:, 0:per, :],) + tuple(ins[1:])
    loads = starts(list(zip(sources, (rows, code, enc, b1, w2, b2, base, wq))), sems)
    loads[1].wait()
    target = lax.broadcasted_iota(jnp.int32, (2 * events, slots), 0) + 1
    sel = jnp.where(target == code[...], 1.0, 0.0)
    back[...] = sel.T.astype(BF16)
    loads[0].wait()
    pair = dotf(sel.astype(BF16), rows[...].reshape(slots, width)).astype(BF16)
    for i in (2, 3):
        loads[i].wait()
    block = 256
    for i in range(hidden.shape[1] // block):
        cut = slice(i * block, (i + 1) * block)
        second = dotf(pair, w1[width : 2 * width, cut])
        third = dotf(enc[...], w1[2 * width :, cut]) + b1[:, cut]
        both = jnp.concatenate([second[events:] + third, second[:events] + third], axis=0)
        hidden[:, cut] = jnp.maximum(dotf(pair, w1[:width, cut]) + both, 0.0).astype(BF16)
    for i in (4, 5):
        loads[i].wait()
    msg = (dotf(hidden[...], w2[...]) + b2[...]).astype(BF16)
    j = lax.broadcasted_iota(jnp.int32, (block, width), 0) & (per - 1)
    loads[6].wait()
    stores = []
    for i in range(slots // block):
        cut = slice(i * block // per, (i + 1) * block // per)
        placed = dotf(back[i * block : (i + 1) * block, :], msg)
        kept = base[cut].reshape(block, width).astype(F32)
        out_v[cut] = jnp.where(j < cap_e, placed, kept).astype(BF16).reshape(block // per, per, width)
        stores.append(pltpu.make_async_copy(out_v.at[cut], out_ref.at[cut], sems.at[8 + i]))
        stores[i].start()
    loads[7].wait()
    q_v[...] = dotf(pair[:events], wq[...]).astype(BF16)
    stores.append(pltpu.make_async_copy(q_v, q_ref, sems.at[7]))
    stores[-1].start()
    for store in stores:
        store.wait()


def messages(cap_e, got, code, w1, enc, b1, w2, b2, base, wq):
    peers, _, width = got.shape
    args = (got, code, enc, b1, w2, b2, base, wq)
    q_shape = (enc.shape[0], width)
    tile = (peers, 8, width)
    anywhere = pl.BlockSpec(memory_space=pl.ANY)
    scratch = [pltpu.VMEM(tile, BF16)] + [pltpu.VMEM(x.shape, x.dtype) for x in args[1:]]
    scratch += [
        pltpu.VMEM((peers * 8, 2 * q_shape[0]), BF16),
        pltpu.VMEM((2 * q_shape[0], w1.shape[1]), BF16),
        pltpu.VMEM(tile, BF16),
        pltpu.VMEM(q_shape, BF16),
        pltpu.SemaphoreType.DMA((9 + peers * 8 // 256,)),
    ]
    return pl.pallas_call(
        functools.partial(message_kernel, cap_e),
        out_shape=(pltpu.HBM(base.shape, BF16), pltpu.HBM(q_shape, BF16)),
        in_specs=[pl.BlockSpec(memory_space=pltpu.VMEM)] + [anywhere] * len(args),
        out_specs=(anywhere, anywhere),
        scratch_shapes=scratch,
        compiler_params=pltpu.CompilerParams(vmem_limit_bytes=28 << 20),
    )(w1, *[hbm(x) for x in args])


def prepare_kernel(old_ref, wh_ref, bias_ref, gh_ref):
    gh_ref[...] = (dotf(old_ref[...], wh_ref[...]) + bias_ref[1:2, :]).astype(BF16)


def prepare(old, wh, bias):
    args = (hbm(old), hbm(wh), hbm(bias))
    shape = (old.shape[0], wh.shape[1])
    return pl.pallas_call(
        prepare_kernel,
        out_shape=pltpu.HBM(shape, BF16),
        grid=(1,),
        in_specs=[whole(x) for x in args],
        out_specs=whole(sds(shape, BF16)),
        compiler_params=pltpu.CompilerParams(vmem_limit_bytes=16 << 20),
    )(*args)


def block_scores(qk_ref, rows, enc, slot_map, events):
    slots, width = rows.shape
    heads = qk_ref.shape[0] // events
    s = lax.dot_general(qk_ref[:, :width], rows, NT, preferred_element_type=F32)
    s = s + lax.dot_general(qk_ref[:, width:], enc, NT, preferred_element_type=F32)
    event = lax.broadcasted_iota(jnp.int32, (events, slots), 0) + 1
    bias = jnp.where(event == slot_map, 0.0, NEG)
    return s + jnp.concatenate([bias] * heads, axis=0)


def block_sums(p, rows, enc):
    slots = rows.shape[0]
    tail = jnp.concatenate([enc, jnp.ones((slots, LANES), BF16)], axis=1)
    return dotf(p, rows), dotf(p, tail)


def attend_kernel(rows_ref, enc_ref, map_ref, q_ref, w_ref, qk_ref, m_ref, a_ref):
    slots, width = rows_ref.shape
    events = q_ref.shape[0]

    @pl.when(pl.program_id(0) == 0)
    def _():
        scale = 1.4426950408889634 / HDIM**0.5
        for h in range(width // HDIM):
            cut = slice(h * HDIM, (h + 1) * HDIM)
            qk = lax.dot_general(q_ref[:, cut], w_ref[:, cut], NT, preferred_element_type=F32)
            qk_ref[h * events : (h + 1) * events, :] = (qk * scale).astype(BF16)
        m_ref[...] = jnp.full(m_ref.shape, NEG, F32)
        a_ref[...] = jnp.zeros(a_ref.shape, F32)

    rows = rows_ref[...]
    enc = enc_ref[...]
    s = block_scores(qk_ref, rows, enc, map_ref[...], events)
    m_old = m_ref[...]
    m = jnp.maximum(m_old, jnp.max(s, axis=1, keepdims=True))
    p = jnp.exp2(s - m[:, 0:1]).astype(BF16)
    scale = jnp.exp2(m_old - m)[:, 0:1]
    m_ref[...] = m
    near, far = block_sums(p, rows, enc)
    a_ref[:, :width] = scale * a_ref[:, :width] + near
    a_ref[:, width:] = scale * a_ref[:, width:] + far


def attend(rows, enc, slot_map, query, w):
    total, width = rows.shape
    block = 1024
    events = query.shape[0]
    stacked = width // HDIM * events
    shapes = (
        ((stacked, width + LANES), BF16),
        ((stacked, LANES), F32),
        ((stacked, width + 2 * LANES), F32),
    )
    return pl.pallas_call(
        attend_kernel,
        out_shape=tuple(pltpu.VMEM(*x) for x in shapes),
        grid=(total // block,),
        in_specs=[
            pl.BlockSpec((block, width), lambda i: (i, 0)),
            pl.BlockSpec((block, LANES), lambda i: (i, 0)),
            pl.BlockSpec((1, block), lambda i: (0, i)),
            whole(query),
            pl.BlockSpec((w.shape[0], width), lambda i: (0, 0)),
        ],
        out_specs=tuple(whole(sds(*x)) for x in shapes),
        compiler_params=pltpu.CompilerParams(vmem_limit_bytes=28 << 20),
    )(hbm(rows), hbm(enc), hbm(slot_map), hbm(query), hbm(w))


def sigmoid(x):
    return 0.5 * jnp.tanh(0.5 * x) + 0.5


def finish_kernel(*refs):
    got, qk, m_prev, a_prev = refs[:4]
    ins = refs[4:16]
    emb_ref, out_ref = refs[16:18]
    (enc, slot_map, to_c, to_t, wi, bias, gh, old, mem, w, wo, to) = refs[18:30]
    tile32, near, gates, emb_v, mem32, fresh32, out_v, sems = refs[30:]
    peers, per, width = got.shape
    slots = old.shape[0]
    cap = slots // peers
    nodes = mem.shape[0]
    parts = width // LANES
    blocks = out_v.shape[0]
    heads = width // HDIM
    events = qk.shape[0] // heads
    sources = list(ins)
    sources[9] = ins[9].at[:, pl.ds(width, width)]
    loads = starts(list(zip(sources, refs[18:30])), sems)
    flat = got[...].reshape(peers * per, width)
    for c in range(parts):
        tile32[c] = flat[:, c * LANES : (c + 1) * LANES].astype(F32)
    for j in range(cap):
        for c in range(parts):
            part = tile32[c, pl.ds(per - cap + j, peers, stride=per), :]
            near[j * peers : (j + 1) * peers, c * LANES : (c + 1) * LANES] = part.astype(BF16)
    for i in range(4):
        loads[i].wait()
    s = block_scores(qk, near[...], enc[...], slot_map[...], events)
    col = jnp.broadcast_to(to_c[...].astype(F32), (8, slots)).T[:, 0:1]
    tiles = to_t[...].astype(F32)
    hits = jnp.where(jnp.logical_and(col == tiles, tiles > 0.0), 1.0, 0.0)
    counts = jnp.sum(hits, axis=1, keepdims=True)
    sums = dotf(hits.astype(BF16), flat)
    m_new = jnp.max(s, axis=1, keepdims=True)
    p = jnp.exp2(s - m_new).astype(BF16)
    mean = (sums * (1.0 / jnp.maximum(counts, 1.0))).astype(BF16)
    for i in range(4, 9):
        loads[i].wait()
    gates[...] = dotf(mean, wi[...]) + bias[0:1, :]
    spread(mem, mem32, parts, static=True)
    rows_sum, tail_sum = block_sums(p, near[...], enc[...])
    block = 128
    for i in range(slots // block):
        at = slice(i * block, (i + 1) * block)
        r = sigmoid(gates[at, :width] + gh[at, :width].astype(F32))
        z = sigmoid(gates[at, width : 2 * width] + gh[at, width : 2 * width].astype(F32))
        c = jnp.tanh(gates[at, 2 * width :] + r * gh[at, 2 * width :].astype(F32))
        fresh = (1.0 - z) * c + z * old[at, :].astype(F32)
        for k in range(parts):
            cut = slice(k * LANES, (k + 1) * LANES)
            fresh32[pl.ds(i * block * parts + k, block, stride=parts), :] = fresh[:, cut]
    for i in range(9, 12):
        loads[i].wait()
    before = m_prev[:, 0:1]
    m = jnp.maximum(m_new, before)
    f_new = jnp.exp2(m_new - m)
    f_old = jnp.exp2(before - m)
    ones_at = width + LANES
    total = f_new * tail_sum[:, LANES : LANES + 1] + f_old * a_prev[:, ones_at : ones_at + 1]
    f_new = f_new / total
    f_old = f_old / total
    mixed_a = (f_new * rows_sum + f_old * a_prev[:, :width]).astype(BF16)
    mixed_b = (f_new * tail_sum[:, :LANES] + f_old * a_prev[:, width:ones_at]).astype(BF16)
    outs = []
    for h in range(heads):
        cut = slice(h * HDIM, (h + 1) * HDIM)
        at = slice(h * events, (h + 1) * events)
        value = dotf(mixed_a[at], w[:width, cut]) + dotf(mixed_b[at], w[width:, cut])
        outs.append(value.astype(BF16))
    emb_v[...] = dotf(jnp.concatenate(outs, axis=1), wo[...]).astype(BF16)
    copies = [pltpu.make_async_copy(emb_v, emb_ref, sems.at[12])]
    copies[0].start()
    for s in range(slots):
        at = pl.multiple_of(to[s], parts)
        mem32[pl.ds(at, parts), :] = fresh32[s * parts : (s + 1) * parts, :]
    size = nodes // blocks
    for b in range(blocks):

        def back(i, carry):
            row = pl.multiple_of(i * 128, 128)
            gather_back(mem32, parts + (b * size + row) * parts, out_v.at[b], row, 128)
            return carry

        lax.fori_loop(0, size // 128, back, 0)
        copy = pltpu.make_async_copy(out_v.at[b], out_ref.at[pl.ds(b * size, size)], sems.at[13 + b])
        copy.start()
        copies.append(copy)
    for copy in copies:
        copy.wait()


def finish(got, qk, m, a, enc, slot_map, to_c, to_t, wi, bias, gh, old, memory, w, wo, to, blocks=4):
    args = (enc, slot_map, to_c, to_t, wi, bias, gh, old, memory, w, wo, to)
    peers, per, width = got.shape
    nodes = memory.shape[0]
    slots = old.shape[0]
    parts = width // LANES
    emb_shape = (qk.shape[0] // (width // HDIM), width)
    anywhere = pl.BlockSpec(memory_space=pl.ANY)
    shapes = [x.shape for x in args[:-1]]
    shapes[9] = (w.shape[0], width)
    scratch = [pltpu.VMEM(shape, x.dtype) for shape, x in zip(shapes, args)]
    scratch += [
        pltpu.SMEM(to.shape, jnp.int32),
        pltpu.VMEM((parts, peers * per, LANES), F32),
        pltpu.VMEM((slots, width), BF16),
        pltpu.VMEM((slots, wi.shape[1]), F32),
        pltpu.VMEM(emb_shape, BF16),
        pltpu.VMEM(((nodes + 1) * parts, LANES), F32),
        pltpu.VMEM((slots * parts, LANES), F32),
        pltpu.VMEM((blocks, nodes // blocks, width), BF16),
        pltpu.SemaphoreType.DMA((13 + blocks,)),
    ]
    return pl.pallas_call(
        finish_kernel,
        out_shape=(pltpu.HBM(emb_shape, BF16), pltpu.HBM(memory.shape, BF16)),
        in_specs=[pl.BlockSpec(memory_space=pltpu.VMEM)] * 4 + [anywhere] * len(args),
        out_specs=(anywhere, anywhere),
        scratch_shapes=scratch,
        compiler_params=pltpu.CompilerParams(vmem_limit_bytes=44 << 20),
    )(got, vmem(qk), vmem(m), vmem(a), *[hbm(x) for x in args])


def encode(dt, freq, phase):
    return jnp.cos(dt[..., None] * freq + phase).astype(BF16)


def on_device(
    memory,
    event_nodes,
    event_ticks,
    neighbour_ids,
    neighbour_ticks,
    freq,
    phase,
    w_msg1,
    b_msg1,
    w_msg2,
    b_msg2,
    w_query,
    w_keyval,
    w_out,
    gru_input,
    gru_hidden,
    gru_bias,
):
    owners = lax.axis_size(AXES)
    nodes, width = memory.shape
    events, fanout = neighbour_ids.shape
    cap_e = 4 * events // owners
    cap_n = 2 * fanout * events // owners
    rows = cap_n + 8
    shift = nodes.bit_length() - 1
    assert nodes == 1 << shift and cap_e == 4 and cap_n == 40
    table = (owners, LANES)
    req, owner_map, dt = call(
        functools.partial(place_kernel, shift, width // LANES, cap_n, rows),
        (sds(table, jnp.int32), sds(table, jnp.int32), sds(table, F32)),
        hbm(neighbour_ids.T),
        hbm(neighbour_ticks.T),
        hbm(event_nodes.T),
        hbm(event_ticks.reshape(1, events)),
        mib=8,
    )
    asked = exchange(req)

    half = 8 - cap_e
    near = cap_n - half
    ev = tuple(range(cap_n, cap_n + cap_e))
    cols_a = ev + tuple(range(near))
    cols_c = tuple(range(near, near + cap_e)) + tuple(range(near, cap_n))
    take = functools.partial(pick, asked, memory)
    sent_a = take(cols_a, static=True, blocks=8)
    got_a = exchange(sent_a)
    base_c = take(cols_c).reshape(owners, -1, width)
    old = take(ev)

    def spaced(x):
        return jnp.concatenate([jnp.zeros((owners, cap_e), x.dtype), x], axis=1)

    def tiled(x):
        return jnp.concatenate([x, jnp.zeros((owners, half), x.dtype)], axis=1).reshape(1, -1)

    code = tiled(owner_map[:, cap_n : cap_n + cap_e])
    map_a = spaced(owner_map[:, :near]).reshape(1, -1)
    map_c = owner_map[:, near:cap_n].T.reshape(1, -1)
    to = asked[:, cap_n : cap_n + cap_e]
    to_s = to.reshape(-1)
    to_c = to.reshape(1, -1)
    to_t = tiled(to)
    gh = prepare(old, gru_hidden, gru_bias)
    enc_a = encode(spaced(dt[:, :near]), freq, phase).reshape(-1, LANES)
    enc_c = encode(dt[:, near:cap_n].T, freq, phase).reshape(-1, LANES)
    enc = encode(event_ticks.astype(F32), freq, phase)
    got_a, enc_a, enc_c, map_a, map_c, to_c, to_t, gh, base_c, to_s = lax.optimization_barrier(
        (got_a, enc_a, enc_c, map_a, map_c, to_c, to_t, gh, base_c, to_s)
    )
    sent_c, query = messages(
        cap_e,
        got_a.reshape(owners, -1, width),
        code,
        w_msg1,
        enc,
        b_msg1.reshape(1, -1),
        w_msg2,
        b_msg2.reshape(1, -1),
        base_c,
        w_query,
    )
    got_c = exchange(sent_c)
    qk, m, a = attend(got_a, enc_a, map_a, query, w_keyval)
    return finish(
        got_c,
        qk,
        m,
        a,
        enc_c,
        map_c,
        to_c,
        to_t,
        gru_input,
        gru_bias,
        gh,
        old,
        memory,
        w_keyval,
        w_out,
        to_s,
    )


def solution(mesh):
    split = P(AXES, None)
    in_specs = (split, split, P(AXES), split, split) + (P(),) * 12
    return jax.shard_map(
        on_device, mesh=mesh, in_specs=in_specs, out_specs=(split, split), check_vma=False
    )
```
